256 devices in a mesh: ctx: 32 (over z, x_lo, core), head: 8 (over x_hi, y).
Axes of the slice: x: 4 (x_hi: 2, x_lo: 2; x = x_hi * 2 + x_lo), y: 4, z: 8, core: 2. Of those that a mesh axis runs over, the one named last changes fastest.
Arguments:
- tokens: bfloat16 [8192, 4096], P('ctx', 'head'), may hold values from -19.8 to 19.8
- query_weight: bfloat16 [4096, 4096], P('ctx', 'head'), may hold values from -0.09375 to 0.09375
- key_weight: bfloat16 [4096, 4096], P('ctx', 'head'), may hold values from -0.09375 to 0.09375
- value_weight: bfloat16 [4096, 4096], P('ctx', 'head'), may hold values from -0.09375 to 0.09375
- output_weight: bfloat16 [4096, 4096], P('ctx', 'head'), may hold values from -0.29882812 to 0.29882812
- adapter_down: bfloat16 [3, 8, 4096], replicated, may hold values from -0.09375 to 0.09375
- adapter_up: bfloat16 [3, 8, 4096], P(None, None, 'head'), may hold values from -0.8984375 to 0.8984375
Outputs:
- attended: bfloat16 [8192, 4096], P('ctx', 'head')
The draws below stay inside these ranges and needn't reach their ends.
All inputs are finite; a program needn't handle non-finite values.
Results may differ from the reference program's by a relative error of at most 0.012.
Values may be sent and summed in bfloat16 or wider, within the bound.
A program may use at most 64 MiB of HBM per device.

```python
import jax
import jax.numpy as jnp
from jax import lax

D = 4096
HEADS = 32
RANK = 8
GROUP_DEV = 16
TOK_DEV = 256
TOKENS = 8192


def common_weight(key):
    normal_part = jax.random.normal(jax.random.fold_in(key, 11), (D, D), jnp.float32)
    return jnp.clip(normal_part, -6.0, 6.0) * D ** (-0.5)


def draw_query_weight(key, part):
    return common_weight(key).astype(jnp.bfloat16)


def draw_key_weight(key, part):
    own_part = jnp.clip(jax.random.normal(jax.random.fold_in(key, 23), (D, D), jnp.float32), -6.0, 6.0) * D ** (-0.5)
    return own_part.astype(jnp.bfloat16)


def draw_tokens(key, part):
    drawn = jnp.clip(jax.random.normal(jax.random.fold_in(key, 31), (TOKENS, D), jnp.float32), -6.0, 6.0)
    return drawn.astype(jnp.bfloat16)


def steps_of(key, dims, split, smallest, high):
    level, own = 1.0, jax.random.fold_in(key, 6)
    for axis_at, blocks in split:
        heights = jnp.exp(jax.random.uniform(jax.random.fold_in(own, axis_at), (blocks,), jnp.float32, smallest / len(split), high / len(split)))
        level = level * jnp.repeat(heights, dims[axis_at] // blocks).reshape([-1 if axis == axis_at else 1 for axis in range(len(dims))])
    return level


def bell_draw(rng, shape, deviation, reach, cuts=(), kind=jnp.bfloat16):
    values = jax.random.normal(rng, shape, jnp.float32) * deviation
    if len(cuts) > 0:
        values = steps_of(rng, shape, cuts, -0.22, 0.18) * values
    return jnp.clip(values, min=-reach, max=reach).astype(kind)


def setup_inputs(seed: int = 0) -> dict:
    key_of = jax.random.split(jax.random.key(seed), 8)
    tokens = draw_tokens(jax.random.fold_in(key_of[7], 71), 0)
    query_weight = draw_query_weight(jax.random.fold_in(key_of[7], 71), 0)
    key_weight = draw_key_weight(jax.random.fold_in(key_of[7], 71), 0)
    value_weight = bell_draw(key_of[3], (D, D), D ** -0.5, 0.09375, ((0, 32), (1, 8)))
    output_weight = bell_draw(key_of[4], (D, D), 0.05, 0.29882812, ((0, 32), (1, 8)))
    adapter_down = bell_draw(key_of[5], (3, RANK, D), D ** -0.5, 0.09375)
    adapter_up = bell_draw(key_of[6], (3, RANK, D), 0.15, 0.8984375, ((2, 8),))
    return {"tokens": tokens, "query_weight": query_weight, "key_weight": key_weight, "value_weight": value_weight, "output_weight": output_weight, "adapter_down": adapter_down, "adapter_up": adapter_up}


def rotary(projection, positions):
    half_dim = projection.shape[-1] // 2
    inverse_freq = 10000.0 ** (-(jnp.arange(half_dim, dtype=jnp.float32) * 2.0) / projection.shape[-1])
    angles = positions.astype(jnp.float32)[:, None] * inverse_freq[None, :]
    cosine = jnp.cos(angles)[:, None, :]
    sine_part = jnp.sin(angles)[:, None, :]
    first_half = projection[..., :half_dim]
    second = projection[..., half_dim:]
    return jnp.concatenate([first_half * cosine - second * sine_part, second * cosine + first_half * sine_part], -1)


def reference(tokens, query_weight, key_weight, value_weight, output_weight, adapter_down, adapter_up):
    head_dim = D // HEADS
    positions = jnp.arange(TOKENS, dtype=jnp.int32)
    projected = []
    for which, weight in enumerate((query_weight, key_weight, value_weight)):
        base_proj = jnp.dot(tokens, weight, preferred_element_type=jnp.float32)
        low_rank = jnp.dot(tokens, adapter_down[which].T, preferred_element_type=jnp.float32).astype(jnp.bfloat16)
        full_proj = base_proj + 2.0 * jnp.dot(low_rank, adapter_up[which], preferred_element_type=jnp.float32)
        projected.append(full_proj.reshape(TOKENS, HEADS, head_dim))
    query = rotary(projected[0], positions).astype(jnp.bfloat16)
    key_rot = rotary(projected[1], positions).astype(jnp.bfloat16)
    value = projected[2].astype(jnp.bfloat16)
    group_size = GROUP_DEV * TOK_DEV
    shift_span = group_size // 2
    shifted = (jnp.arange(HEADS) >= HEADS // 2)[None, :, None]

    def rolled(array, amount):
        return jnp.where(shifted, jnp.roll(array, amount, axis=0), array)

    groups = TOKENS // group_size

    def arrange(array):
        array = rolled(array, -shift_span)
        return array.reshape(groups, group_size, HEADS, head_dim).transpose(0, 2, 1, 3).reshape(groups * HEADS, group_size, head_dim)

    causal = jnp.arange(group_size)[:, None] >= jnp.arange(group_size)[None, :]
    scale = head_dim ** -0.5

    def attend(triple):
        query_blk, key_blk, value_blk = triple
        scores = jnp.dot(query_blk, key_blk.T, preferred_element_type=jnp.float32) * scale
        scores = jnp.where(causal, scores, -1e30)
        row_max = jnp.max(scores, axis=-1, keepdims=True)
        weights = jnp.where(causal, jnp.exp(scores - row_max), 0.0)
        denominator = jnp.sum(weights, axis=-1, keepdims=True)
        result = jnp.dot(weights.astype(jnp.bfloat16), value_blk, preferred_element_type=jnp.float32) / denominator
        return result.astype(jnp.bfloat16)

    outputs = lax.map(attend, (arrange(query), arrange(key_rot), arrange(value)))
    outputs = outputs.reshape(groups, HEADS, group_size, head_dim).transpose(0, 2, 1, 3).reshape(TOKENS, HEADS, head_dim)
    merged = rolled(outputs, shift_span).reshape(TOKENS, D)
    return jnp.dot(merged, output_weight, preferred_element_type=jnp.float32).astype(jnp.bfloat16)
```

```python
import functools

import jax
import jax.numpy as jnp
from jax import lax
from jax.experimental import pallas as pl
from jax.experimental.pallas import tpu as pltpu
from jax.sharding import PartitionSpec as P

D = 4096
HEADS = 32
HEAD = 128
TOK = 256
MESH = pl.DeviceIdType.MESH
BF16 = jnp.bfloat16
F32 = jnp.float32


class Place:
    def __init__(self):
        c = lax.axis_index("ctx")
        h = lax.axis_index("head")
        self.z = lax.div(c, 4)
        self.xl = lax.rem(lax.div(c, 2), 2)
        self.k = lax.rem(c, 2)
        self.xh = lax.div(h, 4)
        self.y = lax.rem(h, 4)
        self.x = self.xh * 2 + self.xl
        self.h = h
        self.sigma = 1 - 2 * self.k

    def at(self, z=None, x=None, y=None, k=None):
        z = self.z if z is None else z
        x = self.x if x is None else x
        y = self.y if y is None else y
        k = self.k if k is None else k
        return (z * 4 + lax.rem(x, 2) * 2 + k, lax.div(x, 2) * 4 + y)

    def to_z(self, step):
        return self.at(z=lax.rem(self.z + 8 + step, 8))

    def to_x(self, step):
        return self.at(x=lax.rem(self.x + 4 + step, 4))

    def to_y(self, step):
        return self.at(y=lax.rem(self.y + 4 + step, 4))

    def sibling(self):
        return self.at(k=1 - self.k)

    def partner(self):
        return self.at(x=self.xh * 2 + 1 - self.xl)


def greet(devices):
    barrier = pltpu.get_barrier_semaphore()
    for device in devices:
        pl.semaphore_signal(barrier, inc=1, device_id=device, device_id_type=MESH)
    pl.semaphore_wait(barrier, len(devices))


class Sends:
    def __init__(self, send_sem, recv_sem):
        self.send_sem, self.recv_sem, self.count, self.open = send_sem, recv_sem, 0, []

    def slot(self):
        self.count += 1
        return self.count - 1

    def start(self, src, dst, device, slot):
        copy = pltpu.make_async_remote_copy(
            src_ref=src,
            dst_ref=dst,
            send_sem=self.send_sem.at[slot],
            recv_sem=self.recv_sem.at[slot],
            device_id=device,
            device_id_type=MESH,
        )
        copy.start()
        self.open.append(copy)
        return copy

    def finish(self):
        for copy in self.open:
            copy.wait_send()


class Ring4:
    def __init__(self, sends, me, sigma, to, block):
        self.sends, self.me, self.sigma, self.to, self.block = sends, me, sigma, to, block

    def place(self, step):
        return self.block(lax.rem(self.me + 4 + step * self.sigma, 4))

    def start(self):
        own = self.place(0)
        self.ahead = self.sends.start(own, own, self.to(self.sigma), self.sends.slot())
        self.back = self.sends.start(own, own, self.to(-self.sigma), self.sends.slot())

    def forward(self):
        self.ahead.wait_recv()
        block = self.place(-1)
        self.far = self.sends.start(block, block, self.to(self.sigma), self.sends.slot())

    def wait_back(self):
        self.back.wait_recv()

    def wait_far(self):
        self.far.wait_recv()


class PlaneGather:
    def __init__(self, sends, me, block):
        self.me, self.sends = me, sends
        s = me.sigma
        self.first = [
            Ring4(sends, me.x, s, me.to_x, lambda a: block(0, a, me.y)),
            Ring4(sends, me.y, s, me.to_y, lambda a: block(1, me.x, a)),
        ]
        self.second = [[], []]
        for step in (0, -1, 1, -2):
            x = lax.rem(me.x + 4 + step * s, 4)
            y = lax.rem(me.y + 4 + step * s, 4)
            self.second[0].append(Ring4(sends, me.y, s, me.to_y, lambda a, x=x: block(0, x, a)))
            self.second[1].append(Ring4(sends, me.x, s, me.to_x, lambda a, y=y: block(1, a, y)))

    def events(self):
        def start():
            for half in (0, 1):
                self.first[half].start()
            for half in (0, 1):
                self.second[half][0].start()

        def ahead():
            for half in (0, 1):
                self.first[half].forward()
                self.second[half][1].start()

        def back():
            for half in (0, 1):
                self.first[half].wait_back()
                self.second[half][2].start()

        def far():
            for half in (0, 1):
                self.first[half].wait_far()
                self.second[half][3].start()

        def second(i):
            def step():
                for half in (0, 1):
                    self.second[half][i].forward()

            return step

        def finish():
            for half in (0, 1):
                for ring in self.second[half]:
                    ring.wait_back()
                    ring.wait_far()

        return [start, ahead, back, second(0), far, second(1), second(2), second(3), finish]


class RingZ:
    def __init__(self, sends, me, block):
        self.sends, self.me, self.block = sends, me, block
        self.ahead, self.back, self.shared = {}, {}, {}

    def place(self, step, k):
        return self.block(lax.rem(self.me.z + 8 + step, 8), k)

    def share(self, key, step):
        block = self.place(step, self.me.k)
        self.shared[key] = self.sends.start(block, block, self.me.sibling(), self.sends.slot())

    def start(self):
        me, own = self.me, self.place(0, self.me.k)
        self.ahead[1] = self.sends.start(own, own, me.to_z(me.sigma), self.sends.slot())
        self.back[1] = self.sends.start(own, own, me.to_z(-me.sigma), self.sends.slot())
        self.share("own", 0)

    def take_ahead(self, s):
        me = self.me
        self.ahead[s].wait_recv()
        if s < 4:
            block = self.place(-s * me.sigma, me.k)
            self.ahead[s + 1] = self.sends.start(block, block, me.to_z(me.sigma), self.sends.slot())
        self.share(("a", s), -s * me.sigma)

    def take_back(self, s):
        me = self.me
        self.back[s].wait_recv()
        if s < 3:
            block = self.place(s * me.sigma, me.k)
            self.back[s + 1] = self.sends.start(block, block, me.to_z(-me.sigma), self.sends.slot())
        self.share(("b", s), s * me.sigma)

    def wait_shared(self, key):
        self.shared[key].wait_recv()


def all_neighbours(me):
    return [
        me.to_z(1),
        me.to_z(-1),
        me.to_x(1),
        me.to_x(-1),
        me.to_y(1),
        me.to_y(-1),
        me.sibling(),
    ]


def project_kernel(
    tok_in, wq_in, wk_in, wv_in, down_ref, up_ref, cos_ref, sin_ref, out_ref,
    tok, weights, acc, low, send_sem, recv_sem, local_sem,
):
    me = Place()
    w_in = (wq_in, wk_in, wv_in)
    own_cols = pl.multiple_of(me.xl * 256, 256)
    other_cols = pl.multiple_of((1 - me.xl) * 256, 256)
    local = [pltpu.make_async_copy(tok_in, tok.at[me.h, me.xl], local_sem.at[0])]
    for j in range(3):
        local.append(
            pltpu.make_async_copy(
                w_in[j].at[:, pl.ds(own_cols, 256)], weights.at[j, me.z, me.xl, me.k], local_sem.at[1 + j]
            )
        )
    for copy in local:
        copy.start()
    greet(all_neighbours(me))
    sends = Sends(send_sem, recv_sem)
    trade = []
    for j in range(3):
        trade.append(
            sends.start(
                w_in[j].at[:, pl.ds(other_cols, 256)],
                weights.at[j, me.z, me.xl, me.k],
                me.partner(),
                sends.slot(),
            )
        )
    for copy in local[1:]:
        copy.wait()
    own_ring = RingZ(sends, me, lambda z, k: weights.at[:, z, me.xl, k])
    other_ring = RingZ(sends, me, lambda z, k: weights.at[:, z, 1 - me.xl, k])
    own_ring.start()
    local[0].wait()

    def block(half, x, y):
        return tok.at[lax.div(x, 2) * 4 + y, lax.rem(x, 2), pl.ds(half * 128, 128)]

    events = PlaneGather(sends, me, block).events()
    events[0]()
    events[1]()
    for copy in trade:
        copy.wait_recv()
    other_ring.start()
    own_ring.take_ahead(1)
    own_ring.take_back(1)
    events[2]()
    events[3]()
    events[4]()
    other_ring.take_ahead(1)
    other_ring.take_back(1)
    events[5]()
    events[6]()
    own_ring.take_ahead(2)
    own_ring.take_back(2)
    events[7]()
    other_ring.take_ahead(2)
    other_ring.take_back(2)
    events[8]()

    def multiply(step, first=False):
        chunk = lax.rem(me.z + 8 + step, 8)
        left = tok[chunk].reshape(512, 512)
        for j in range(3):
            part = jnp.dot(left, weights[j, chunk].reshape(512, 256), preferred_element_type=F32)
            if first:
                acc[j] = part
            else:
                acc[j] += part

    def low_rank(chunk, total):
        left = tok[chunk].reshape(512, 512)
        cols = pl.multiple_of(chunk * 512, 512)
        return total + lax.dot_general(
            left, down_ref[:, pl.ds(cols, 512)], (((1,), (1,)), ((), ())), preferred_element_type=F32
        )

    def shared(key):
        own_ring.wait_shared(key)
        other_ring.wait_shared(key)

    shared("own")
    multiply(0, True)
    low[...] = lax.fori_loop(0, 4, low_rank, jnp.zeros((512, 24), F32))
    own_ring.take_ahead(3)
    own_ring.take_back(3)
    for s in (1, 2):
        shared(("a", s))
        shared(("b", s))
        multiply(s)
        multiply(-s)
    other_ring.take_ahead(3)
    other_ring.take_back(3)
    own_ring.take_ahead(4)
    low[...] = lax.fori_loop(4, 8, low_rank, low[...])
    shared(("a", 3))
    shared(("b", 3))
    multiply(3)
    multiply(-3)
    other_ring.take_ahead(4)
    shared(("a", 4))
    multiply(4)
    rank = low[...].astype(BF16)
    rank_of = lax.broadcasted_iota(jnp.int32, (512, 24), 1) // 8
    for j in range(3):
        mine = jnp.where(rank_of == j, rank, jnp.zeros_like(rank))
        full = acc[j] + 2.0 * jnp.dot(mine, up_ref[:, pl.ds(own_cols, 256)], preferred_element_type=F32)
        for head in range(2):
            part = full[:, head * HEAD : (head + 1) * HEAD]
            if j < 2:
                part = part * cos_ref[...] + pltpu.roll(part, HEAD // 2, 1) * sin_ref[...]
            out_ref[head, j] = part.astype(BF16)
    sends.finish()


def project(tokens, wq, wk, wv, down, up, cosine, sine):
    slots = 64
    any_spec = pl.BlockSpec(memory_space=pl.ANY)
    vmem = pl.BlockSpec(memory_space=pltpu.VMEM)
    return pl.pallas_call(
        project_kernel,
        out_shape=jax.ShapeDtypeStruct((2, 3, 2 * TOK, HEAD), BF16),
        in_specs=[any_spec] * 4 + [vmem] * 4,
        out_specs=vmem,
        scratch_shapes=[
            pltpu.VMEM((8, 2, TOK, 512), BF16),
            pltpu.VMEM((3, 8, 2, 2, 128, 256), BF16),
            pltpu.VMEM((3, 512, 256), F32),
            pltpu.VMEM((512, 24), F32),
            pltpu.SemaphoreType.DMA((slots + 1,)),
            pltpu.SemaphoreType.DMA((slots + 1,)),
            pltpu.SemaphoreType.DMA((4,)),
        ],
        compiler_params=pltpu.CompilerParams(
            collective_id=0, has_side_effects=True, vmem_limit_bytes=40 << 20
        ),
        name="project",
    )(tokens, wq, wk, wv, down, up, cosine, sine)


def attend_kernel(qkv_in, out_ref, query, kv, total, top, denom, far_out, send_sem, recv_sem, local_sem):
    me = Place()
    p = lax.rem(me.z + 8 - 2 * me.xh, 4)
    mine = lax.div(p, 2)
    own_slot = mine
    lower = p + mine * (3 - 2 * p)

    def plane(q):
        return me.at(z=lax.rem(me.z + 8 - p + q, 8))

    def receive_q():
        return pltpu.make_async_remote_copy(
            qkv_in.at[0, 0], query.at[1 - own_slot], send_sem.at[0], recv_sem.at[0],
            device_id=me.sibling(), device_id_type=MESH,
        )

    local = [
        pltpu.make_async_copy(qkv_in.at[mine, 0], query.at[own_slot], local_sem.at[0]),
        pltpu.make_async_copy(qkv_in.at[mine, pl.ds(1, 2)], kv.at[p, me.k], local_sem.at[1]),
    ]
    for copy in local:
        copy.start()
    greet([plane(lax.rem(p + 1, 4)), plane(lax.rem(p + 2, 4)), plane(lax.rem(p + 3, 4)), me.sibling()])

    def kv_copy(src, b, device, send):
        return pltpu.make_async_remote_copy(
            src, kv.at[b, me.k], send_sem.at[send], recv_sem.at[1 + b],
            device_id=device, device_id_type=MESH,
        )

    def q_copy(head, slot, device):
        return pltpu.make_async_remote_copy(
            qkv_in.at[head, 0], query.at[slot], send_sem.at[0], recv_sem.at[0],
            device_id=device, device_id_type=MESH,
        )

    def kv_in(head):
        return qkv_in.at[head, pl.ds(1, 2)]

    def share(b, src):
        return pltpu.make_async_remote_copy(
            src, kv.at[b, me.k], send_sem.at[5 + b], recv_sem.at[5 + b],
            device_id=me.sibling(), device_id_type=MESH,
        )

    @pl.when(p == 0)
    def _():
        kv_copy(kv_in(0), 0, plane(1), 1).start()
        kv_copy(kv_in(1), 0, plane(2), 2).start()
        q_copy(1, 0, plane(3)).start()

    @pl.when(p == 1)
    def _():
        kv_copy(kv_in(1), 1, plane(2), 2).start()
        q_copy(1, 0, plane(2)).start()
        kv_copy(kv_in(0), 1, plane(0), 1).start()

    @pl.when(p == 2)
    def _():
        kv_copy(kv_in(0), 2, plane(1), 1).start()
        q_copy(0, 1, plane(1)).start()
        kv_copy(kv_in(1), 2, plane(3), 2).start()

    @pl.when(p == 3)
    def _():
        q_copy(0, 1, plane(0)).start()
        kv_copy(kv_in(0), 3, plane(0), 1).start()

    share(p, kv_in(mine)).start()
    top[...] = jnp.full_like(top, -1e30)
    denom[...] = jnp.zeros_like(denom)
    total[...] = jnp.zeros_like(total)
    for copy in local:
        copy.wait()

    rows = lax.broadcasted_iota(jnp.int32, (TOK, 512), 0)
    cols = lax.broadcasted_iota(jnp.int32, (TOK, 512), 1)
    key_place = lax.div(cols, 256) * 512 + lax.rem(cols, 256)
    scale = HEAD ** (-0.5)

    def update(slot, b, half, core, masked):
        q = query[slot, pl.ds(half * TOK, TOK)]
        scores = lax.dot_general(
            q, kv[b, core, 0], (((1,), (1,)), ((), ())), preferred_element_type=F32
        ) * scale
        if masked:
            allowed = key_place + core * 256 <= rows + half * 512 + me.k * 256
            scores = jnp.where(allowed, scores, -1e30)
        part = pl.ds(half * TOK, TOK)
        old = top[slot, part]
        new = jnp.maximum(old, jnp.max(scores, axis=1, keepdims=True))
        weights = jnp.exp(scores - new)
        if masked:
            weights = jnp.where(allowed, weights, 0.0)
        factor = jnp.exp(old - new)
        top[slot, part] = new
        denom[slot, part] = denom[slot, part] * factor + jnp.sum(weights, axis=1, keepdims=True)
        total[slot, part] = total[slot, part] * factor + jnp.dot(
            weights.astype(BF16), kv[b, core, 1], preferred_element_type=F32
        )

    def block_of(slot):
        return lower + slot * (3 - 2 * lower)

    def pair(slot, b):
        @pl.when(block_of(slot) > b)
        def _():
            for half in range(2):
                for core in range(2):
                    update(slot, b, half, core, False)

        @pl.when(block_of(slot) == b)
        def _():
            for half in range(2):
                for core in range(2):
                    update(slot, b, half, core, True)

    def step(t, carry):
        b = jnp.where(
            p == 0, t, jnp.where(p == 3, 3 - t, jnp.where(p == 1, lax.rem(t + 1, 3), 2 - t))
        )
        used = (p == 0) | (p == 3) | (t < 3)

        @pl.when(used & (t > 0))
        def _():
            kv_copy(kv.at[b, me.k], b, me.sibling(), 1).wait_recv()
            share(b, kv.at[b, me.k]).start()

            @pl.when((p == 1) & (b == 2))
            def _():
                kv_copy(kv.at[2, me.k], 2, plane(0), 3).start()

            @pl.when(p == 2)
            def _():
                kv_copy(kv.at[b, me.k], b, plane(3), 3 + lax.rem(b, 2)).start()

        @pl.when(t == 1)
        def _():
            receive_q().wait_recv()

        @pl.when(used)
        def _():
            share(b, kv.at[b, me.k]).wait_recv()
            own_first = jnp.where(t == 0, own_slot, 0)
            count = jnp.where(t == 0, 1, 2)

            def slots(i, c):
                pair(own_first + i, b)
                return c

            lax.fori_loop(0, count, slots, 0)

            @pl.when((t == 1) & (block_of(1 - own_slot) >= p))
            def _():
                pair(1 - own_slot, p)

        return carry

    lax.fori_loop(0, 4, step, 0)
    for slot in range(2):
        result = (total[slot] / denom[slot]).astype(BF16)
        far_out[slot] = result
    give = pltpu.make_async_remote_copy(
        far_out.at[1 - own_slot], out_ref.at[mine], send_sem.at[9], recv_sem.at[9],
        device_id=plane(3 - p), device_id_type=MESH,
    )
    give.start()
    out_ref[mine] = far_out[own_slot]
    q_copy(0, 0, me.sibling()).wait_send()
    kv_copy(kv_in(0), 0, me.sibling(), 1).wait_send()

    @pl.when(p < 3)
    def _():
        kv_copy(kv_in(0), 0, me.sibling(), 2).wait_send()

    @pl.when(p == 1)
    def _():
        kv_copy(kv_in(0), 0, me.sibling(), 3).wait_send()

    @pl.when(p == 2)
    def _():
        kv_copy(kv_in(0), 0, me.sibling(), 3).wait_send()
        kv_copy(kv_in(0), 0, me.sibling(), 4).wait_send()

    for b in range(3):
        share(b, kv_in(0)).wait_send()

    @pl.when((p == 0) | (p == 3))
    def _():
        share(3, kv_in(0)).wait_send()

    give.wait()


def attend(qkv):
    vmem = pl.BlockSpec(memory_space=pltpu.VMEM)
    return pl.pallas_call(
        attend_kernel,
        out_shape=jax.ShapeDtypeStruct((2, 2 * TOK, HEAD), BF16),
        in_specs=[pl.BlockSpec(memory_space=pl.ANY)],
        out_specs=vmem,
        scratch_shapes=[
            pltpu.VMEM((2, 512, HEAD), BF16),
            pltpu.VMEM((4, 2, 2, 512, HEAD), BF16),
            pltpu.VMEM((2, 512, HEAD), F32),
            pltpu.VMEM((2, 512, 1), F32),
            pltpu.VMEM((2, 512, 1), F32),
            pltpu.VMEM((2, 512, HEAD), BF16),
            pltpu.SemaphoreType.DMA((10,)),
            pltpu.SemaphoreType.DMA((10,)),
            pltpu.SemaphoreType.DMA((2,)),
        ],
        compiler_params=pltpu.CompilerParams(
            collective_id=1, has_side_effects=True, vmem_limit_bytes=40 << 20
        ),
        name="attend",
    )(qkv)


def merge_kernel(
    heads_in, wo_in, out_ref, merged, weights, acc, stage, send_sem, recv_sem, local_sem
):
    me = Place()
    own_cols = pl.multiple_of(me.xl * 256, 256)
    other_cols = pl.multiple_of((1 - me.xl) * 256, 256)
    local = [
        pltpu.make_async_copy(heads_in, merged.at[me.h, me.xl], local_sem.at[0]),
        pltpu.make_async_copy(
            wo_in.at[:, pl.ds(own_cols, 256)], weights.at[me.z, me.xl, me.k], local_sem.at[1]
        ),
    ]
    for copy in local:
        copy.start()
    greet(all_neighbours(me))
    sends = Sends(send_sem, recv_sem)
    trade = sends.start(
        wo_in.at[:, pl.ds(other_cols, 256)],
        weights.at[me.z, me.xl, me.k],
        me.partner(),
        sends.slot(),
    )
    for copy in local:
        copy.wait()

    def block(half, x, y):
        return merged.at[lax.div(x, 2) * 4 + y, lax.rem(x, 2), half]

    events = PlaneGather(sends, me, block).events()
    ring = RingZ(sends, me, lambda z, k: weights.at[z, :, k])
    events[0]()
    trade.wait_recv()
    ring.start()
    events[1]()
    events[2]()
    ring.take_ahead(1)
    ring.take_back(1)
    events[3]()
    events[4]()
    ring.take_ahead(2)
    ring.take_back(2)
    events[5]()
    ring.take_ahead(3)
    ring.take_back(3)
    events[6]()
    ring.take_ahead(4)
    events[7]()
    ring.wait_shared("own")
    for s in (1, 2, 3):
        ring.wait_shared(("a", s))
        ring.wait_shared(("b", s))
    ring.wait_shared(("a", 4))
    events[8]()

    def multiply(h, total):
        for xl in range(2):
            left = jnp.concatenate([merged[h, xl, 0], merged[h, xl, 1]], axis=1)
            total = total + jnp.dot(
                left, weights[h, xl].reshape(256, 256), preferred_element_type=F32
            )
        return total

    acc[...] = jnp.zeros_like(acc)

    @pl.loop(0, 8)
    def _(h):
        acc[...] = multiply(h, acc[...])

    stage[0] = acc[pl.ds(0, TOK)].astype(BF16)
    stage[1] = acc[pl.ds(TOK, TOK)].astype(BF16)
    give = sends.start(
        stage.at[1 - me.xl], out_ref.at[:, pl.ds(own_cols, 256)], me.partner(), sends.slot()
    )
    out_ref[:, pl.ds(own_cols, 256)] = stage[me.xl]
    give.wait_recv()
    sends.finish()


def merge(heads, wo):
    any_spec = pl.BlockSpec(memory_space=pl.ANY)
    vmem = pl.BlockSpec(memory_space=pltpu.VMEM)
    return pl.pallas_call(
        merge_kernel,
        out_shape=jax.ShapeDtypeStruct((TOK, 512), BF16),
        in_specs=[any_spec] * 2,
        out_specs=vmem,
        scratch_shapes=[
            pltpu.VMEM((8, 2, 2, 512, HEAD), BF16),
            pltpu.VMEM((8, 2, 2, 128, 256), BF16),
            pltpu.VMEM((512, 256), F32),
            pltpu.VMEM((2, TOK, 256), BF16),
            pltpu.SemaphoreType.DMA((64,)),
            pltpu.SemaphoreType.DMA((64,)),
            pltpu.SemaphoreType.DMA((2,)),
        ],
        compiler_params=pltpu.CompilerParams(
            collective_id=2, has_side_effects=True, vmem_limit_bytes=40 << 20
        ),
        name="merge",
    )(heads, wo)


def rotary_tables():
    c = lax.axis_index("ctx")
    base = lax.div(c, 4) * 1024 + lax.rem(c, 2) * 256
    rows = jnp.arange(512, dtype=jnp.int32)
    positions = base + (rows // 256) * 512 + rows % 256
    inverse_freq = 10000.0 ** (-(jnp.arange(HEAD // 2, dtype=F32) * 2.0) / HEAD)
    angles = positions.astype(F32)[:, None] * inverse_freq[None, :]
    cosine, sine = jnp.cos(angles), jnp.sin(angles)
    return jnp.concatenate([cosine, cosine], 1), jnp.concatenate([-sine, sine], 1)


def per_device(tokens, wq, wk, wv, wo, down, up):
    cosine, sine = rotary_tables()
    qkv = project(tokens, wq, wk, wv, down.reshape(24, D), up.reshape(24, 512), cosine, sine)
    heads = attend(qkv)
    return merge(heads, wo)


def solution(mesh):
    placed = P("ctx", "head")
    return jax.shard_map(
        per_device,
        mesh=mesh,
        in_specs=(placed,) * 5 + (P(), P(None, None, "head")),
        out_specs=placed,
        check_vma=False,
    )
```

```python
import functools

import jax
import jax.numpy as jnp
from jax import lax
from jax.experimental import pallas as pl
from jax.experimental.pallas import tpu as pltpu
from jax.sharding import PartitionSpec as P

D = 4096
HEADS = 32
HEAD = 128
TOK = 256
MESH = pl.DeviceIdType.MESH
BF16 = jnp.bfloat16
F32 = jnp.float32


class Place:
    def __init__(self):
        c = lax.axis_index("ctx")
        h = lax.axis_index("head")
        self.z = lax.div(c, 4)
        self.xl = lax.rem(lax.div(c, 2), 2)
        self.k = lax.rem(c, 2)
        self.xh = lax.div(h, 4)
        self.y = lax.rem(h, 4)
        self.x = self.xh * 2 + self.xl
        self.h = h
        self.sigma = 1 - 2 * self.k

    def at(self, z=None, x=None, y=None, k=None):
        z = self.z if z is None else z
        x = self.x if x is None else x
        y = self.y if y is None else y
        k = self.k if k is None else k
        return (z * 4 + lax.rem(x, 2) * 2 + k, lax.div(x, 2) * 4 + y)

    def to_z(self, step):
        return self.at(z=lax.rem(self.z + 8 + step, 8))

    def to_x(self, step):
        return self.at(x=lax.rem(self.x + 4 + step, 4))

    def to_y(self, step):
        return self.at(y=lax.rem(self.y + 4 + step, 4))

    def sibling(self):
        return self.at(k=1 - self.k)

    def partner(self):
        return self.at(x=self.xh * 2 + 1 - self.xl)


def greet(devices):
    barrier = pltpu.get_barrier_semaphore()
    for device in devices:
        pl.semaphore_signal(barrier, inc=1, device_id=device, device_id_type=MESH)
    pl.semaphore_wait(barrier, len(devices))


class Sends:
    def __init__(self, send_sem, recv_sem):
        self.send_sem, self.recv_sem, self.count, self.open = send_sem, recv_sem, 0, []

    def slot(self):
        self.count += 1
        return self.count - 1

    def start(self, src, dst, device, slot):
        copy = pltpu.make_async_remote_copy(
            src_ref=src,
            dst_ref=dst,
            send_sem=self.send_sem.at[slot],
            recv_sem=self.recv_sem.at[slot],
            device_id=device,
            device_id_type=MESH,
        )
        copy.start()
        self.open.append(copy)
        return copy

    def finish(self):
        for copy in self.open:
            copy.wait_send()


class Ring4:
    def __init__(self, sends, me, sigma, to, block):
        self.sends, self.me, self.sigma, self.to, self.block = sends, me, sigma, to, block

    def place(self, step):
        return self.block(lax.rem(self.me + 4 + step * self.sigma, 4))

    def start(self):
        own = self.place(0)
        self.ahead = self.sends.start(own, own, self.to(self.sigma), self.sends.slot())
        self.back = self.sends.start(own, own, self.to(-self.sigma), self.sends.slot())

    def forward(self):
        self.ahead.wait_recv()
        block = self.place(-1)
        self.far = self.sends.start(block, block, self.to(self.sigma), self.sends.slot())

    def wait_back(self):
        self.back.wait_recv()

    def wait_far(self):
        self.far.wait_recv()


class PlaneGather:
    def __init__(self, sends, me, block):
        self.me, self.sends = me, sends
        s = me.sigma
        self.first = [
            Ring4(sends, me.x, s, me.to_x, lambda a: block(0, a, me.y)),
            Ring4(sends, me.y, s, me.to_y, lambda a: block(1, me.x, a)),
        ]
        self.second = [[], []]
        for step in (0, -1, 1, -2):
            x = lax.rem(me.x + 4 + step * s, 4)
            y = lax.rem(me.y + 4 + step * s, 4)
            self.second[0].append(Ring4(sends, me.y, s, me.to_y, lambda a, x=x: block(0, x, a)))
            self.second[1].append(Ring4(sends, me.x, s, me.to_x, lambda a, y=y: block(1, a, y)))

    def events(self):
        def start():
            for half in (0, 1):
                self.first[half].start()
            for half in (0, 1):
                self.second[half][0].start()

        def ahead():
            for half in (0, 1):
                self.first[half].forward()
                self.second[half][1].start()

        def back():
            for half in (0, 1):
                self.first[half].wait_back()
                self.second[half][2].start()

        def far():
            for half in (0, 1):
                self.first[half].wait_far()
                self.second[half][3].start()

        def second(i):
            def step():
                for half in (0, 1):
                    self.second[half][i].forward()

            return step

        def finish():
            for half in (0, 1):
                for ring in self.second[half]:
                    ring.wait_back()
                    ring.wait_far()

        return [start, ahead, back, second(0), far, second(1), second(2), second(3), finish]


class HeadGather:
    def __init__(self, sends, me, block):
        self.me, self.sends, self.block = me, sends, block
        far = 1 - me.xh
        self.own_a = Ring4(sends, me.y, me.sigma, me.to_y, lambda a: block(0, me.xh, a))
        self.far_a = Ring4(sends, me.y, me.sigma, me.to_y, lambda a: block(0, far, a))
        self.own_b = Ring4(sends, me.y, me.sigma, me.to_y, lambda a: block(1, me.xh, a))
        self.crossed = []

    def cross(self, half, step):
        block = self.block(half, self.me.xh, lax.rem(self.me.y + 4 + step * self.me.sigma, 4))
        self.crossed.append(
            self.sends.start(block, block, self.me.to_x(2), self.sends.slot())
        )

    def start(self):
        self.cross(0, 0)
        self.own_b.start()
        self.cross(1, 0)
        self.own_a.start()

    def step_1(self):
        self.own_b.forward()
        self.cross(1, -1)
        self.own_b.wait_back()
        self.cross(1, 1)

    def step_2(self):
        self.crossed[0].wait_recv()
        self.far_a.start()
        self.own_a.forward()

    def step_3(self):
        self.own_b.wait_far()
        self.cross(1, -2)
        self.far_a.forward()

    def finish(self):
        for ring in (self.own_a, self.far_a):
            ring.wait_back()
            ring.wait_far()
        for copy in self.crossed[1:]:
            copy.wait_recv()


class RingZ:
    def __init__(self, sends, me, block):
        self.sends, self.me, self.block = sends, me, block
        self.ahead, self.back, self.shared = {}, {}, {}

    def place(self, step, k):
        return self.block(lax.rem(self.me.z + 8 + step, 8), k)

    def share(self, key, step):
        block = self.place(step, self.me.k)
        self.shared[key] = self.sends.start(block, block, self.me.sibling(), self.sends.slot())

    def start(self):
        me, own = self.me, self.place(0, self.me.k)
        self.ahead[1] = self.sends.start(own, own, me.to_z(me.sigma), self.sends.slot())
        self.back[1] = self.sends.start(own, own, me.to_z(-me.sigma), self.sends.slot())
        self.share("own", 0)

    def take_ahead(self, s):
        me = self.me
        self.ahead[s].wait_recv()
        if s < 4:
            block = self.place(-s * me.sigma, me.k)
            self.ahead[s + 1] = self.sends.start(block, block, me.to_z(me.sigma), self.sends.slot())
        self.share(("a", s), -s * me.sigma)

    def take_back(self, s):
        me = self.me
        self.back[s].wait_recv()
        if s < 3:
            block = self.place(s * me.sigma, me.k)
            self.back[s + 1] = self.sends.start(block, block, me.to_z(-me.sigma), self.sends.slot())
        self.share(("b", s), s * me.sigma)

    def wait_shared(self, key):
        self.shared[key].wait_recv()


def layer_kernel(
    tok_in, wq_in, wk_in, wv_in, wo_in, down_ref, up_ref, cos_ref, sin_ref, out_ref,
    tok, weights, acc, low, qkv, query, kv, total, top, denom, heads_out, merged, wo,
    send_sem, recv_sem, pair_send, pair_recv, local_sem,
):
    me = Place()
    w_in = (wq_in, wk_in, wv_in)
    own_cols = pl.multiple_of(me.xl * 256, 256)
    other_cols = pl.multiple_of((1 - me.xl) * 256, 256)
    p = lax.rem(me.z + 8 - 2 * me.xh, 4)
    mine = lax.div(p, 2)
    lower = p + mine * (3 - 2 * p)

    def plane(q, x=None):
        return me.at(z=lax.rem(me.z + 8 - p + q, 8), x=x)

    partner_x = me.xh * 2 + 1 - me.xl
    local = [pltpu.make_async_copy(tok_in, tok.at[me.h, me.xl], local_sem.at[0])]
    for j in range(3):
        local.append(
            pltpu.make_async_copy(
                w_in[j].at[:, pl.ds(own_cols, 256)], weights.at[j, me.z, me.xl, me.k], local_sem.at[1 + j]
            )
        )
    local.append(pltpu.make_async_copy(wo_in, wo.at[me.z, me.xl, me.k], local_sem.at[4]))
    for copy in local:
        copy.start()
    greet(
        [
            me.to_z(1), me.to_z(-1), me.to_x(1), me.to_x(-1), me.to_x(2), me.to_y(1), me.to_y(-1), me.sibling(),
            plane(lax.rem(p + 1, 4)), plane(lax.rem(p + 2, 4)), plane(lax.rem(p + 3, 4)), plane(3 - p, partner_x),
        ]
    )
    sends = Sends(send_sem, recv_sem)
    trade = []
    for j in range(3):
        trade.append(
            sends.start(
                w_in[j].at[:, pl.ds(other_cols, 256)],
                weights.at[j, me.z, me.xl, me.k],
                me.partner(),
                sends.slot(),
            )
        )
    for copy in local[1:]:
        copy.wait()
    own_ring = RingZ(sends, me, lambda z, k: weights.at[:, z, me.xl, k])
    other_ring = RingZ(sends, me, lambda z, k: weights.at[:, z, 1 - me.xl, k])
    own_ring.start()
    local[0].wait()

    def block(half, x, y):
        return tok.at[lax.div(x, 2) * 4 + y, lax.rem(x, 2), pl.ds(half * 128, 128)]

    events = PlaneGather(sends, me, block).events()
    events[0]()
    events[1]()
    for copy in trade:
        copy.wait_recv()
    other_ring.start()
    own_ring.take_ahead(1)
    own_ring.take_back(1)
    events[2]()
    events[3]()
    events[4]()
    other_ring.take_ahead(1)
    other_ring.take_back(1)
    events[5]()
    events[6]()
    own_ring.take_ahead(2)
    own_ring.take_back(2)
    events[7]()
    other_ring.take_ahead(2)
    other_ring.take_back(2)
    events[8]()
    trade_wo = sends.start(
        wo.at[me.z, me.xl, me.k], wo.at[me.z, me.xl, me.k], me.partner(), sends.slot()
    )

    def multiply(step, first=False):
        chunk = lax.rem(me.z + 8 + step, 8)
        left = tok[chunk].reshape(512, 512)
        for j in (1, 2, 0):
            part = jnp.dot(left, weights[j, chunk].reshape(512, 256), preferred_element_type=F32)
            if first:
                acc[j] = part
            else:
                acc[j] += part

    def low_rank(chunk, so_far):
        left = tok[chunk].reshape(512, 512)
        cols = pl.multiple_of(chunk * 512, 512)
        return so_far + lax.dot_general(
            left, down_ref[:, pl.ds(cols, 512)], (((1,), (1,)), ((), ())), preferred_element_type=F32
        )

    def shared(key):
        own_ring.wait_shared(key)
        other_ring.wait_shared(key)

    shared("own")
    multiply(0, True)
    low[...] = lax.fori_loop(0, 4, low_rank, jnp.zeros((512, 24), F32))
    own_ring.take_ahead(3)
    own_ring.take_back(3)
    for s in (1, 2):
        shared(("a", s))
        shared(("b", s))
        multiply(s)
        multiply(-s)
    other_ring.take_ahead(3)
    other_ring.take_back(3)
    own_ring.take_ahead(4)
    low[...] = lax.fori_loop(4, 8, low_rank, low[...])
    shared(("a", 3))
    shared(("b", 3))
    multiply(3)
    multiply(-3)
    top[...] = jnp.full_like(top, -1e30)
    denom[...] = jnp.zeros_like(denom)
    total[...] = jnp.zeros_like(total)
    other_ring.take_ahead(4)
    shared(("a", 4))
    multiply(4)
    rank = low[...].astype(BF16)
    rank_of = lax.broadcasted_iota(jnp.int32, (512, 24), 1) // 8

    def finish_projection(j):
        part_rank = jnp.where(rank_of == j, rank, jnp.zeros_like(rank))
        full = acc[j] + 2.0 * jnp.dot(
            part_rank, up_ref[:, pl.ds(own_cols, 256)], preferred_element_type=F32
        )
        for head in range(2):
            part = full[:, head * HEAD : (head + 1) * HEAD]
            if j < 2:
                part = part * cos_ref[...] + pltpu.roll(part, HEAD // 2, 1) * sin_ref[...]
            qkv[head, j] = part.astype(BF16)

    def kv_copy(src, b, device, send):
        return pltpu.make_async_remote_copy(
            src, kv.at[b, me.k], pair_send.at[send], pair_recv.at[1 + b],
            device_id=device, device_id_type=MESH,
        )

    def q_copy(head, slot, device):
        return pltpu.make_async_remote_copy(
            qkv.at[head, 0], query.at[slot], pair_send.at[0], pair_recv.at[0],
            device_id=device, device_id_type=MESH,
        )

    def kv_of(head):
        return qkv.at[head, pl.ds(1, 2)]

    def share(b, src):
        return pltpu.make_async_remote_copy(
            src, kv.at[b, me.k], pair_send.at[5 + b], pair_recv.at[5 + b],
            device_id=me.sibling(), device_id_type=MESH,
        )

    finish_projection(1)
    finish_projection(2)

    @pl.when(p == 0)
    def _():
        kv_copy(kv_of(0), 0, plane(1), 1).start()
        kv_copy(kv_of(1), 0, plane(2), 2).start()

    @pl.when(p == 1)
    def _():
        kv_copy(kv_of(1), 1, plane(2), 2).start()

    @pl.when(p == 2)
    def _():
        kv_copy(kv_of(0), 2, plane(1), 1).start()

    share(p, kv_of(mine)).start()
    finish_projection(0)

    @pl.when(p == 0)
    def _():
        q_copy(1, 0, plane(3)).start()

    @pl.when(p == 1)
    def _():
        q_copy(1, 0, plane(2)).start()
        kv_copy(kv_of(0), 1, plane(0), 1).start()

    @pl.when(p == 2)
    def _():
        q_copy(0, 1, plane(1)).start()
        kv_copy(kv_of(1), 2, plane(3), 2).start()

    @pl.when(p == 3)
    def _():
        q_copy(0, 1, plane(0)).start()
        kv_copy(kv_of(0), 3, plane(0), 1).start()

    query[mine] = qkv[mine, 0]
    kv[p, me.k] = qkv[mine, 1:3]
    rows = lax.broadcasted_iota(jnp.int32, (TOK, 512), 0)
    cols = lax.broadcasted_iota(jnp.int32, (TOK, 512), 1)
    key_place = lax.div(cols, 256) * 512 + lax.rem(cols, 256)
    scale = HEAD ** (-0.5)

    def update(slot, b, half, core, masked):
        q = query[slot, pl.ds(half * TOK, TOK)]
        scores = lax.dot_general(
            q, kv[b, core, 0], (((1,), (1,)), ((), ())), preferred_element_type=F32
        ) * scale
        if masked:
            allowed = key_place + core * 256 <= rows + half * 512 + me.k * 256
            scores = jnp.where(allowed, scores, -1e30)
        part = pl.ds(half * TOK, TOK)
        old = top[slot, part]
        new = jnp.maximum(old, jnp.max(scores, axis=1, keepdims=True))
        probs = jnp.exp(scores - new)
        if masked:
            probs = jnp.where(allowed, probs, 0.0)
        factor = jnp.exp(old - new)
        top[slot, part] = new
        denom[slot, part] = denom[slot, part] * factor + jnp.sum(probs, axis=1, keepdims=True)
        total[slot, part] = total[slot, part] * factor + jnp.dot(
            probs.astype(BF16), kv[b, core, 1], preferred_element_type=F32
        )

    def block_of(slot):
        return lower + slot * (3 - 2 * lower)

    def pair(slot, b):
        @pl.when(block_of(slot) > b)
        def _():
            for half in range(2):
                for core in range(2):
                    update(slot, b, half, core, False)

        @pl.when(block_of(slot) == b)
        def _():
            for half in range(2):
                for core in range(2):
                    update(slot, b, half, core, True)

    def step(t, carry):
        b = jnp.where(
            p == 0, t, jnp.where(p == 3, 3 - t, jnp.where(p == 1, lax.rem(t + 1, 3), 2 - t))
        )
        used = (p == 0) | (p == 3) | (t < 3)

        @pl.when(used & (t > 0))
        def _():
            kv_copy(kv.at[b, me.k], b, me.sibling(), 1).wait_recv()
            share(b, kv.at[b, me.k]).start()

            @pl.when((p == 1) & (b == 2))
            def _():
                kv_copy(kv.at[2, me.k], 2, plane(0), 3).start()

            @pl.when(p == 2)
            def _():
                kv_copy(kv.at[b, me.k], b, plane(3), 3 + lax.rem(b, 2)).start()

        @pl.when(t == 1)
        def _():
            q_copy(0, 1 - mine, me.sibling()).wait_recv()

        @pl.when(used)
        def _():
            share(b, kv.at[b, me.k]).wait_recv()
            first = jnp.where(t == 0, mine, 0)
            count = jnp.where(t == 0, 1, 2)

            def slots(i, c):
                pair(first + i, b)
                return c

            lax.fori_loop(0, count, slots, 0)

            @pl.when((t == 1) & (block_of(1 - mine) >= p))
            def _():
                pair(1 - mine, p)

        return carry

    lax.fori_loop(0, 4, step, 0)
    trade_wo.wait_recv()
    ring_a = RingZ(sends, me, lambda z, k: wo.at[z, me.xl, k])
    ring_b = RingZ(sends, me, lambda z, k: wo.at[z, 1 - me.xl, k])
    give = []
    place = merged.at[me.h, me.xl * 2 + mine]

    far_slot = 1 - mine
    heads_out[far_slot] = (total[far_slot] / denom[far_slot]).astype(BF16)
    for x, r in ((me.x, me.xl), (partner_x, 1 - me.xl)):
        rows_r = pl.ds(pl.multiple_of(r * TOK, TOK), TOK)
        give.append(sends.start(heads_out.at[far_slot, rows_r], place, plane(3 - p, x), sends.slot()))
    heads_out[mine] = (total[mine] / denom[mine]).astype(BF16)
    rows_r = pl.ds(pl.multiple_of((1 - me.xl) * TOK, TOK), TOK)
    give.append(sends.start(heads_out.at[mine, rows_r], place, me.partner(), sends.slot()))
    merged[me.h, me.xl * 2 + mine] = heads_out[mine, pl.ds(pl.multiple_of(me.xl * TOK, TOK), TOK)]
    ring_a.start()
    ring_b.start()

    for copy in give:
        copy.wait_recv()
    gather = HeadGather(sends, me, lambda half, xh, y: merged.at[xh * 4 + y, pl.ds(half * 2, 2)])
    gather.start()
    ring_a.take_ahead(1)
    ring_a.take_back(1)
    gather.step_1()
    ring_b.take_ahead(1)
    ring_b.take_back(1)
    gather.step_2()
    ring_a.take_ahead(2)
    ring_a.take_back(2)
    gather.step_3()
    ring_b.take_ahead(2)
    ring_b.take_back(2)
    ring_a.take_ahead(3)
    ring_a.take_back(3)
    ring_b.take_ahead(3)
    ring_b.take_back(3)
    gather.finish()

    def merge(step, so_far):
        h = lax.rem(me.z + 8 + step, 8)
        for half in range(2):
            left = jnp.concatenate([merged[h, 2 * half], merged[h, 2 * half + 1]], axis=1)
            so_far = so_far + jnp.dot(
                left, wo[h, half].reshape(256, 512), preferred_element_type=F32
            )
        return so_far

    def ready(key):
        ring_a.wait_shared(key)
        ring_b.wait_shared(key)

    ready("own")
    result = merge(0, jnp.zeros((TOK, 512), F32))
    for s in (1, 2):
        ready(("a", s))
        ready(("b", s))
        result = merge(-s, merge(s, result))
    ring_a.take_ahead(4)
    ready(("a", 3))
    ready(("b", 3))
    result = merge(-3, merge(3, result))
    ring_b.take_ahead(4)
    ready(("a", 4))
    out_ref[...] = merge(4, result).astype(BF16)

    q_copy(0, 0, me.sibling()).wait_send()
    kv_copy(kv_of(0), 0, me.sibling(), 1).wait_send()

    @pl.when(p < 3)
    def _():
        kv_copy(kv_of(0), 0, me.sibling(), 2).wait_send()

    @pl.when(p == 1)
    def _():
        kv_copy(kv_of(0), 0, me.sibling(), 3).wait_send()

    @pl.when(p == 2)
    def _():
        kv_copy(kv_of(0), 0, me.sibling(), 3).wait_send()
        kv_copy(kv_of(0), 0, me.sibling(), 4).wait_send()

    for b in range(3):
        share(b, kv_of(0)).wait_send()

    @pl.when((p == 0) | (p == 3))
    def _():
        share(3, kv_of(0)).wait_send()

    sends.finish()


def layer(tokens, wq, wk, wv, wo, down, up, cosine, sine):
    slots = 120
    any_spec = pl.BlockSpec(memory_space=pl.ANY)
    vmem = pl.BlockSpec(memory_space=pltpu.VMEM)
    return pl.pallas_call(
        layer_kernel,
        out_shape=jax.ShapeDtypeStruct((TOK, 512), BF16),
        in_specs=[any_spec] * 5 + [vmem] * 4,
        out_specs=vmem,
        scratch_shapes=[
            pltpu.VMEM((8, 2, TOK, 512), BF16),
            pltpu.VMEM((3, 8, 2, 2, 128, 256), BF16),
            pltpu.VMEM((3, 512, 256), F32),
            pltpu.VMEM((512, 24), F32),
            pltpu.VMEM((2, 3, 512, HEAD), BF16),
            pltpu.VMEM((2, 512, HEAD), BF16),
            pltpu.VMEM((4, 2, 2, 512, HEAD), BF16),
            pltpu.VMEM((2, 512, HEAD), F32),
            pltpu.VMEM((2, 512, 1), F32),
            pltpu.VMEM((2, 512, 1), F32),
            pltpu.VMEM((2, 512, HEAD), BF16),
            pltpu.VMEM((8, 4, TOK, HEAD), BF16),
            pltpu.VMEM((8, 2, 2, 128, 512), BF16),
            pltpu.SemaphoreType.DMA((slots,)),
            pltpu.SemaphoreType.DMA((slots,)),
            pltpu.SemaphoreType.DMA((9,)),
            pltpu.SemaphoreType.DMA((9,)),
            pltpu.SemaphoreType.DMA((5,)),
        ],
        compiler_params=pltpu.CompilerParams(
            collective_id=0, has_side_effects=True, vmem_limit_bytes=48 << 20
        ),
        name="layer",
    )(tokens, wq, wk, wv, wo, down, up, cosine, sine)


def rotary_tables():
    c = lax.axis_index("ctx")
    base = lax.div(c, 4) * 1024 + lax.rem(c, 2) * 256
    rows = jnp.arange(512, dtype=jnp.int32)
    positions = base + (rows // 256) * 512 + rows % 256
    inverse_freq = 10000.0 ** (-(jnp.arange(HEAD // 2, dtype=F32) * 2.0) / HEAD)
    angles = positions.astype(F32)[:, None] * inverse_freq[None, :]
    cosine, sine = jnp.cos(angles), jnp.sin(angles)
    return jnp.concatenate([cosine, cosine], 1), jnp.concatenate([-sine, sine], 1)


def per_device(tokens, wq, wk, wv, wo, down, up):
    cosine, sine = rotary_tables()
    return layer(tokens, wq, wk, wv, wo, down.reshape(24, D), up.reshape(24, 512), cosine, sine)


def solution(mesh):
    placed = P("ctx", "head")
    return jax.shard_map(
        per_device,
        mesh=mesh,
        in_specs=(placed,) * 5 + (P(), P(None, None, "head")),
        out_specs=placed,
        check_vma=False,
    )
```

```python
import functools

import jax
import jax.numpy as jnp
from jax import lax
from jax.experimental import pallas as pl
from jax.experimental.pallas import tpu as pltpu
from jax.sharding import PartitionSpec as P

D = 4096
HEADS = 32
HEAD = 128
TOK = 256
MESH = pl.DeviceIdType.MESH
BF16 = jnp.bfloat16
F32 = jnp.float32


class Place:
    def __init__(self):
        c = lax.axis_index("ctx")
        h = lax.axis_index("head")
        self.z = lax.div(c, 4)
        self.xl = lax.rem(lax.div(c, 2), 2)
        self.k = lax.rem(c, 2)
        self.xh = lax.div(h, 4)
        self.y = lax.rem(h, 4)
        self.x = self.xh * 2 + self.xl
        self.h = h
        self.sigma = 1 - 2 * self.k

    def at(self, z=None, x=None, y=None, k=None):
        z = self.z if z is None else z
        x = self.x if x is None else x
        y = self.y if y is None else y
        k = self.k if k is None else k
        return (z * 4 + lax.rem(x, 2) * 2 + k, lax.div(x, 2) * 4 + y)

    def to_z(self, step):
        return self.at(z=lax.rem(self.z + 8 + step, 8))

    def to_x(self, step):
        return self.at(x=lax.rem(self.x + 4 + step, 4))

    def to_y(self, step):
        return self.at(y=lax.rem(self.y + 4 + step, 4))

    def sibling(self):
        return self.at(k=1 - self.k)

    def partner(self):
        return self.at(x=self.xh * 2 + 1 - self.xl)


def greet(devices):
    barrier = pltpu.get_barrier_semaphore()
    for device in devices:
        pl.semaphore_signal(barrier, inc=1, device_id=device, device_id_type=MESH)
    pl.semaphore_wait(barrier, len(devices))


class Sends:
    def __init__(self, send_sem, recv_sem):
        self.send_sem, self.recv_sem, self.count, self.open = send_sem, recv_sem, 0, []

    def slot(self):
        self.count += 1
        return self.count - 1

    def start(self, src, dst, device, slot):
        copy = pltpu.make_async_remote_copy(
            src_ref=src,
            dst_ref=dst,
            send_sem=self.send_sem.at[slot],
            recv_sem=self.recv_sem.at[slot],
            device_id=device,
            device_id_type=MESH,
        )
        copy.start()
        self.open.append(copy)
        return copy

    def finish(self):
        for copy in self.open:
            copy.wait_send()


class Ring4:
    def __init__(self, sends, me, sigma, to, block):
        self.sends, self.me, self.sigma, self.to, self.block = sends, me, sigma, to, block

    def place(self, step):
        return self.block(lax.rem(self.me + 4 + step * self.sigma, 4))

    def start(self):
        own = self.place(0)
        self.ahead = self.sends.start(own, own, self.to(self.sigma), self.sends.slot())
        self.back = self.sends.start(own, own, self.to(-self.sigma), self.sends.slot())

    def forward(self):
        self.ahead.wait_recv()
        block = self.place(-1)
        self.far = self.sends.start(block, block, self.to(self.sigma), self.sends.slot())

    def wait_back(self):
        self.back.wait_recv()

    def wait_far(self):
        self.far.wait_recv()


class PlaneGather:
    def __init__(self, sends, me, block):
        self.me, self.sends = me, sends
        s = me.sigma
        self.first = [
            Ring4(sends, me.x, s, me.to_x, lambda a: block(0, a, me.y)),
            Ring4(sends, me.y, s, me.to_y, lambda a: block(1, me.x, a)),
        ]
        self.second = [[], []]
        for step in (0, -1, 1, -2):
            x = lax.rem(me.x + 4 + step * s, 4)
            y = lax.rem(me.y + 4 + step * s, 4)
            self.second[0].append(Ring4(sends, me.y, s, me.to_y, lambda a, x=x: block(0, x, a)))
            self.second[1].append(Ring4(sends, me.x, s, me.to_x, lambda a, y=y: block(1, a, y)))

    def events(self):
        def start():
            for half in (0, 1):
                self.first[half].start()
            for half in (0, 1):
                self.second[half][0].start()

        def ahead():
            for half in (0, 1):
                self.first[half].forward()
                self.second[half][1].start()

        def back():
            for half in (0, 1):
                self.first[half].wait_back()
                self.second[half][2].start()

        def far():
            for half in (0, 1):
                self.first[half].wait_far()
                self.second[half][3].start()

        def second(i):
            def step():
                for half in (0, 1):
                    self.second[half][i].forward()

            return step

        def finish():
            for half in (0, 1):
                for ring in self.second[half]:
                    ring.wait_back()
                    ring.wait_far()

        return [start, ahead, back, second(0), far, second(1), second(2), second(3), finish]


class HeadGather:
    def __init__(self, sends, me, block):
        self.me, self.sends, self.block = me, sends, block
        far = 1 - me.xh
        self.own_a = Ring4(sends, me.y, me.sigma, me.to_y, lambda a: block(0, me.xh, a))
        self.far_a = Ring4(sends, me.y, me.sigma, me.to_y, lambda a: block(0, far, a))
        self.own_b = Ring4(sends, me.y, me.sigma, me.to_y, lambda a: block(1, me.xh, a))
        self.crossed = []

    def cross(self, half, step):
        block = self.block(half, self.me.xh, lax.rem(self.me.y + 4 + step * self.me.sigma, 4))
        self.crossed.append(
            self.sends.start(block, block, self.me.to_x(2), self.sends.slot())
        )

    def start(self):
        self.cross(0, 0)
        self.own_b.start()
        self.cross(1, 0)
        self.own_a.start()

    def step_1(self):
        self.own_b.forward()
        self.cross(1, -1)
        self.own_b.wait_back()
        self.cross(1, 1)

    def step_2(self):
        self.crossed[0].wait_recv()
        self.far_a.start()
        self.own_a.forward()

    def step_3(self):
        self.own_b.wait_far()
        self.cross(1, -2)
        self.far_a.forward()

    def finish(self):
        for ring in (self.own_a, self.far_a):
            ring.wait_back()
            ring.wait_far()
        for copy in self.crossed[1:]:
            copy.wait_recv()


class RingZ:
    def __init__(self, sends, me, block):
        self.sends, self.me, self.block = sends, me, block
        self.ahead, self.back, self.shared = {}, {}, {}

    def place(self, step, k):
        return self.block(lax.rem(self.me.z + 8 + step, 8), k)

    def share(self, key, step):
        block = self.place(step, self.me.k)
        self.shared[key] = self.sends.start(block, block, self.me.sibling(), self.sends.slot())

    def start(self):
        me, own = self.me, self.place(0, self.me.k)
        self.ahead[1] = self.sends.start(own, own, me.to_z(me.sigma), self.sends.slot())
        self.back[1] = self.sends.start(own, own, me.to_z(-me.sigma), self.sends.slot())
        self.share("own", 0)

    def take_ahead(self, s):
        me = self.me
        self.ahead[s].wait_recv()
        if s < 4:
            block = self.place(-s * me.sigma, me.k)
            self.ahead[s + 1] = self.sends.start(block, block, me.to_z(me.sigma), self.sends.slot())
        self.share(("a", s), -s * me.sigma)

    def take_back(self, s):
        me = self.me
        self.back[s].wait_recv()
        if s < 3:
            block = self.place(s * me.sigma, me.k)
            self.back[s + 1] = self.sends.start(block, block, me.to_z(-me.sigma), self.sends.slot())
        self.share(("b", s), s * me.sigma)

    def wait_shared(self, key):
        self.shared[key].wait_recv()


def layer_kernel(
    tok_in, wq_in, wk_in, wv_in, wo_in, down_ref, up_ref, cos_ref, sin_ref, out_ref,
    tok, weights, acc, low, qkv, query, kv, total, top, denom, heads_out, merged, wo,
    send_sem, recv_sem, pair_send, pair_recv, hand_send, hand_recv, local_sem,
):
    me = Place()
    w_in = (wq_in, wk_in, wv_in)
    own_cols = pl.multiple_of(me.xl * 256, 256)
    other_cols = pl.multiple_of((1 - me.xl) * 256, 256)
    p = lax.rem(me.z + 8 - 2 * me.xh, 4)
    mine = lax.div(p, 2)
    last = lax.rem(p, 2)

    def plane(q, x=None):
        return me.at(z=lax.rem(me.z + 8 - p + q, 8), x=x)

    partner_x = me.xh * 2 + 1 - me.xl
    local = [pltpu.make_async_copy(tok_in, tok.at[me.h, me.xl], local_sem.at[0])]
    for j in range(3):
        local.append(
            pltpu.make_async_copy(
                w_in[j].at[:, pl.ds(own_cols, 256)], weights.at[j, me.z, me.xl, me.k], local_sem.at[1 + j]
            )
        )
    local.append(pltpu.make_async_copy(wo_in, wo.at[me.z, me.xl, me.k], local_sem.at[4]))
    for copy in local:
        copy.start()
    greet(
        [
            me.to_z(1), me.to_z(-1), me.to_x(1), me.to_x(-1), me.to_x(2), me.to_y(1), me.to_y(-1), me.sibling(),
            plane(lax.rem(p + 1, 4)), plane(lax.rem(p + 2, 4)), plane(lax.rem(p + 3, 4)),
            plane(lax.rem(p + 1, 4), partner_x), plane(lax.rem(p + 2, 4), partner_x), plane(lax.rem(p + 3, 4), partner_x),
        ]
    )
    sends = Sends(send_sem, recv_sem)
    trade = []
    for j in range(3):
        trade.append(
            sends.start(
                w_in[j].at[:, pl.ds(other_cols, 256)],
                weights.at[j, me.z, me.xl, me.k],
                me.partner(),
                sends.slot(),
            )
        )
    for copy in local[1:]:
        copy.wait()
    own_ring = RingZ(sends, me, lambda z, k: weights.at[:, z, me.xl, k])
    other_ring = RingZ(sends, me, lambda z, k: weights.at[:, z, 1 - me.xl, k])
    own_ring.start()
    local[0].wait()

    def block(half, x, y):
        return tok.at[lax.div(x, 2) * 4 + y, lax.rem(x, 2), pl.ds(half * 128, 128)]

    events = PlaneGather(sends, me, block).events()
    events[0]()
    events[1]()
    for copy in trade:
        copy.wait_recv()
    other_ring.start()
    own_ring.take_ahead(1)
    own_ring.take_back(1)
    events[2]()
    events[3]()
    events[4]()
    other_ring.take_ahead(1)
    other_ring.take_back(1)
    events[5]()
    events[6]()
    own_ring.take_ahead(2)
    own_ring.take_back(2)
    events[7]()
    other_ring.take_ahead(2)
    other_ring.take_back(2)
    events[8]()
    trade_wo = sends.start(
        wo.at[me.z, me.xl, me.k], wo.at[me.z, me.xl, me.k], me.partner(), sends.slot()
    )

    def multiply(step, first=False):
        chunk = lax.rem(me.z + 8 + step, 8)
        left = tok[chunk].reshape(512, 512)
        for j in (1, 2, 0):
            part = jnp.dot(left, weights[j, chunk].reshape(512, 256), preferred_element_type=F32)
            if first:
                acc[j] = part
            else:
                acc[j] += part

    def low_rank(chunk, so_far):
        left = tok[chunk].reshape(512, 512)
        cols = pl.multiple_of(chunk * 512, 512)
        return so_far + lax.dot_general(
            left, down_ref[:, pl.ds(cols, 512)], (((1,), (1,)), ((), ())), preferred_element_type=F32
        )

    def shared(key):
        own_ring.wait_shared(key)
        other_ring.wait_shared(key)

    shared("own")
    multiply(0, True)
    low[...] = lax.fori_loop(0, 4, low_rank, jnp.zeros((512, 24), F32))
    own_ring.take_ahead(3)
    own_ring.take_back(3)
    for s in (1, 2):
        shared(("a", s))
        shared(("b", s))
        multiply(s)
        multiply(-s)
    other_ring.take_ahead(3)
    other_ring.take_back(3)
    own_ring.take_ahead(4)
    rank = lax.fori_loop(4, 8, low_rank, low[...]).astype(BF16)
    rank_of = lax.broadcasted_iota(jnp.int32, (512, 24), 1) // 8
    for j in range(3):
        part_rank = jnp.where(rank_of == j, rank, jnp.zeros_like(rank))
        acc[j] += 2.0 * jnp.dot(
            part_rank, up_ref[:, pl.ds(own_cols, 256)], preferred_element_type=F32
        )
    shared(("a", 3))
    shared(("b", 3))
    multiply(3)
    multiply(-3)
    top[...] = jnp.full_like(top, -1e30)
    denom[...] = jnp.zeros_like(denom)
    total[...] = jnp.zeros_like(total)
    other_ring.take_ahead(4)
    shared(("a", 4))
    multiply(4)

    def finish_projection(j):
        for head in range(2):
            part = acc[j, :, head * HEAD : (head + 1) * HEAD]
            if j < 2:
                part = part * cos_ref[...] + pltpu.roll(part, HEAD // 2, 1) * sin_ref[...]
            qkv[head, j] = part.astype(BF16)

    def kv_copy(src, b, device, send):
        return pltpu.make_async_remote_copy(
            src, kv.at[b, me.k], pair_send.at[send], pair_recv.at[b],
            device_id=device, device_id_type=MESH,
        )

    def q_copy(head, b, device, send):
        return pltpu.make_async_remote_copy(
            qkv.at[head, 0], query.at[b], pair_send.at[send], pair_recv.at[4 + b],
            device_id=device, device_id_type=MESH,
        )

    def kv_of(head):
        return qkv.at[head, pl.ds(1, 2)]

    def share(b, src):
        return pltpu.make_async_remote_copy(
            src, kv.at[b, me.k], pair_send.at[8 + b], pair_recv.at[8 + b],
            device_id=me.sibling(), device_id_type=MESH,
        )

    finish_projection(1)
    finish_projection(2)

    @pl.when(p == 0)
    def _():
        kv_copy(kv_of(0), 0, plane(1), 1).start()

    @pl.when(p == 1)
    def _():
        kv_copy(kv_of(1), 1, plane(2), 1).start()

    @pl.when(p == 2)
    def _():
        kv_copy(kv_of(0), 2, plane(1), 0).start()
        kv_copy(kv_of(1), 2, plane(3), 1).start()

    share(p, kv_of(mine)).start()
    finish_projection(0)

    @pl.when(p == 1)
    def _():
        q_copy(0, 1, plane(0), 2).start()
        kv_copy(kv_of(0), 1, plane(0), 0).start()

    @pl.when(p != 1)
    def _():
        query[p] = qkv[mine, 0]

    kv[p, me.k] = qkv[mine, 1:3]
    ring_a = RingZ(sends, me, lambda z, k: wo.at[z, me.xl, k])
    ring_b = RingZ(sends, me, lambda z, k: wo.at[z, 1 - me.xl, k])
    scale = HEAD ** (-0.5)

    def allowed(half, core, keys):
        rows = lax.broadcasted_iota(jnp.int32, (TOK, keys), 0)
        cols = lax.broadcasted_iota(jnp.int32, (TOK, keys), 1)
        place = cols + jnp.where(cols >= TOK, 256, 0)
        return place + core * 256 <= rows + half * 512 + me.k * 256

    def pair(slot, b, diagonal):
        for half in range(2):
            part = pl.ds(half * TOK, TOK)
            keys = TOK if diagonal and half == 0 else 2 * TOK
            q = query[slot, part]
            scores = []
            for core in range(2):
                score = lax.dot_general(
                    q, kv[b, core, 0, pl.ds(0, keys)], (((1,), (1,)), ((), ())), preferred_element_type=F32
                ) * scale
                if diagonal:
                    score = jnp.where(allowed(half, core, keys), score, -1e30)
                scores.append(score)
            old = top[slot, part]
            new = jnp.maximum(old, jnp.max(jnp.maximum(scores[0], scores[1]), axis=1, keepdims=True))
            probs = [jnp.exp(score - new) for score in scores]
            if diagonal:
                probs = [
                    jnp.where(allowed(half, core, keys), probs[core], 0.0) for core in range(2)
                ]
            factor = jnp.exp(old - new)
            top[slot, part] = new
            denom[slot, part] = denom[slot, part] * factor + jnp.sum(
                probs[0] + probs[1], axis=1, keepdims=True
            )
            result = total[slot, part] * factor
            for core in range(2):
                result = result + jnp.dot(
                    probs[core].astype(BF16),
                    kv[b, core, 1, pl.ds(0, keys)],
                    preferred_element_type=F32,
                )
            total[slot, part] = result

    def arrive(b, onward=None):
        kv_copy(kv.at[b, me.k], b, me.sibling(), 0).wait_recv()
        if onward is not None:
            kv_copy(kv.at[b, me.k], b, plane(onward), 4 + b).start()
        share(b, kv.at[b, me.k]).start()

    def got_query(b):
        q_copy(0, b, me.sibling(), 2).wait_recv()

    def whole(b):
        share(b, kv.at[b, me.k]).wait_recv()

    def pairs(first, count, b):
        def one(i, c):
            pair(first + i, b, False)
            return c

        lax.fori_loop(0, count, one, 0)

    whole(p)

    @pl.when(p != 1)
    def _():
        pair(p, p, True)

    one = 1 + last

    @pl.when(p == 0)
    def _():
        kv_copy(kv_of(0), 0, me.sibling(), 1).wait_send()
        kv_copy(kv_of(1), 0, plane(2), 0).start()
        arrive(1)
        got_query(1)

    @pl.when(p == 1)
    def _():
        arrive(2, 0)
        got_query(3)
        q_copy(1, 1, plane(2), 3).start()

    @pl.when(p == 2)
    def _():
        arrive(1, 3)
        kv_copy(kv_of(0), 2, me.sibling(), 0).wait_send()
        q_copy(0, 2, plane(0), 2).start()

    @pl.when(p == 3)
    def _():
        arrive(2)
        q_copy(0, 3, plane(1), 2).start()
        kv_copy(kv_of(0), 3, plane(1), 0).start()

    whole(one)

    @pl.when(p == 0)
    def _():
        pair(1, 1, True)

    def second(i, c):
        q = jnp.where(p == 0, 1, jnp.where(p == 2, 2, 3))
        b = jnp.where(p == 0, 0, jnp.where(p == 1, 1 + i, jnp.where(p == 2, 1, 2)))
        pair(q, b, False)
        return c

    lax.fori_loop(0, jnp.where(p == 1, 2, 1), second, 0)

    @pl.when(p == 0)
    def _():
        kv_copy(kv_of(1), 0, me.sibling(), 0).wait_send()
        q_copy(1, 0, plane(2), 2).start()
        got_query(2)

    @pl.when(p == 1)
    def _():
        arrive(0)

    @pl.when(p == 2)
    def _():
        arrive(0, 3)
        got_query(1)

    @pl.when(p == 3)
    def _():
        arrive(1)

    @pl.when(p != 0)
    def _():
        whole(jnp.where(p == 3, 1, 0))

    def third(i, c):
        q = jnp.where(p == 0, 2, jnp.where(p == 2, 1 + i, 3))
        b = jnp.where(p == 0, i, jnp.where(p == 3, 1, 0))
        pair(q, b, False)
        return c

    lax.fori_loop(0, 2 - last, third, 0)

    @pl.when(p == 0)
    def _():
        arrive(2)
        whole(2)

    @pl.when(p == 1)
    def _():
        arrive(3)
        whole(3)

    @pl.when(p == 2)
    def _():
        got_query(0)

    def own_keys(i, c):
        q = jnp.where(p == 0, 2, jnp.where(p == 1, 3, 1 - i))
        pair(q, q, True)
        return c

    @pl.when(p != 3)
    def _():
        lax.fori_loop(0, jnp.where(p == 2, 2, 1), own_keys, 0)

    @pl.when(p == 3)
    def _():
        arrive(0)
        whole(0)
        pair(3, 0, False)

    def rows_of(r):
        return pl.ds(pl.multiple_of(r * TOK, TOK), TOK)

    place = merged.at[me.h, me.xl * 2 + mine]

    def hand_copy(b, r, x, column):
        return pltpu.make_async_remote_copy(
            heads_out.at[b, rows_of(r)], place, hand_send.at[2 * b + column], hand_recv.at[2 * mine + column],
            device_id=plane(b, x), device_id_type=MESH,
        )

    def hand_over(b):
        heads_out[b] = (total[b] / denom[b]).astype(BF16)
        hand_copy(b, 1 - me.xl, partner_x, 1).start()

        @pl.when(b != p)
        def _():
            hand_copy(b, me.xl, me.x, 0).start()

        @pl.when(b == p)
        def _():
            merged[me.h, me.xl * 2 + mine] = heads_out[p, rows_of(me.xl)]

    @pl.when(last == 1)
    def _():
        hand_over(3)

    @pl.when(last == 0)
    def _():
        for b in (1, 0, 2):
            hand_over(b)

    trade_wo.wait_recv()
    ring_a.start()
    ring_b.start()
    for head in range(2):
        pltpu.make_async_remote_copy(
            heads_out.at[0, pl.ds(0, TOK)], place, hand_send.at[0], hand_recv.at[2 * head + 1],
            device_id=me.sibling(), device_id_type=MESH,
        ).wait_recv()
        here = (p == 0) if head == 0 else (p >= 2)

        @pl.when(jnp.logical_not(here))
        def _():
            pltpu.make_async_remote_copy(
                heads_out.at[0, pl.ds(0, TOK)], place, hand_send.at[0], hand_recv.at[2 * head],
                device_id=me.sibling(), device_id_type=MESH,
            ).wait_recv()

    gather = HeadGather(sends, me, lambda half, xh, y: merged.at[xh * 4 + y, pl.ds(half * 2, 2)])
    gather.start()
    ring_a.take_ahead(1)
    ring_a.take_back(1)
    gather.step_1()
    ring_b.take_ahead(1)
    ring_b.take_back(1)
    gather.step_2()
    ring_a.take_ahead(2)
    ring_a.take_back(2)
    gather.step_3()
    ring_b.take_ahead(2)
    ring_b.take_back(2)
    ring_a.take_ahead(3)
    ring_a.take_back(3)
    ring_b.take_ahead(3)
    ring_b.take_back(3)
    gather.finish()

    def merge(step, so_far):
        h = lax.rem(me.z + 8 + step, 8)
        for half in range(2):
            left = jnp.concatenate([merged[h, 2 * half], merged[h, 2 * half + 1]], axis=1)
            so_far = so_far + jnp.dot(
                left, wo[h, half].reshape(256, 512), preferred_element_type=F32
            )
        return so_far

    def ready(key):
        ring_a.wait_shared(key)
        ring_b.wait_shared(key)

    ready("own")
    result = merge(0, jnp.zeros((TOK, 512), F32))
    for s in (1, 2):
        ready(("a", s))
        ready(("b", s))
        result = merge(-s, merge(s, result))
    ring_a.take_ahead(4)
    ready(("a", 3))
    ready(("b", 3))
    result = merge(-3, merge(3, result))
    ring_b.take_ahead(4)
    ready(("a", 4))
    out_ref[...] = merge(4, result).astype(BF16)

    q_copy(0, 0, me.sibling(), 2).wait_send()

    @pl.when(last == 1)
    def _():
        kv_copy(kv_of(0), 0, me.sibling(), 0).wait_send()

    @pl.when((p == 1) | (p == 2))
    def _():
        kv_copy(kv_of(0), 0, me.sibling(), 1).wait_send()

    @pl.when(p == 1)
    def _():
        q_copy(0, 0, me.sibling(), 3).wait_send()
        kv_copy(kv_of(0), 0, me.sibling(), 6).wait_send()

    @pl.when(p == 2)
    def _():
        kv_copy(kv_of(0), 0, me.sibling(), 4).wait_send()
        kv_copy(kv_of(0), 0, me.sibling(), 5).wait_send()

    for b in range(3):
        share(b, kv_of(0)).wait_send()

    @pl.when(last == 1)
    def _():
        share(3, kv_of(0)).wait_send()
        hand_copy(3, 0, partner_x, 1).wait_send()

    @pl.when(p == 1)
    def _():
        hand_copy(3, 0, me.x, 0).wait_send()

    @pl.when(last == 0)
    def _():
        for b in range(3):
            hand_copy(b, 0, partner_x, 1).wait_send()

            @pl.when(b != p)
            def _():
                hand_copy(b, 0, me.x, 0).wait_send()

    sends.finish()


def layer(tokens, wq, wk, wv, wo, down, up, cosine, sine):
    slots = 120
    any_spec = pl.BlockSpec(memory_space=pl.ANY)
    vmem = pl.BlockSpec(memory_space=pltpu.VMEM)
    return pl.pallas_call(
        layer_kernel,
        out_shape=jax.ShapeDtypeStruct((TOK, 512), BF16),
        in_specs=[any_spec] * 5 + [vmem] * 4,
        out_specs=vmem,
        scratch_shapes=[
            pltpu.VMEM((8, 2, TOK, 512), BF16),
            pltpu.VMEM((3, 8, 2, 2, 128, 256), BF16),
            pltpu.VMEM((3, 512, 256), F32),
            pltpu.VMEM((512, 24), F32),
            pltpu.VMEM((2, 3, 512, HEAD), BF16),
            pltpu.VMEM((4, 512, HEAD), BF16),
            pltpu.VMEM((4, 2, 2, 512, HEAD), BF16),
            pltpu.VMEM((4, 512, HEAD), F32),
            pltpu.VMEM((4, 512, 1), F32),
            pltpu.VMEM((4, 512, 1), F32),
            pltpu.VMEM((4, 512, HEAD), BF16),
            pltpu.VMEM((8, 4, TOK, HEAD), BF16),
            pltpu.VMEM((8, 2, 2, 128, 512), BF16),
            pltpu.SemaphoreType.DMA((slots,)),
            pltpu.SemaphoreType.DMA((slots,)),
            pltpu.SemaphoreType.DMA((12,)),
            pltpu.SemaphoreType.DMA((12,)),
            pltpu.SemaphoreType.DMA((8,)),
            pltpu.SemaphoreType.DMA((4,)),
            pltpu.SemaphoreType.DMA((5,)),
        ],
        compiler_params=pltpu.CompilerParams(
            collective_id=0, has_side_effects=True, vmem_limit_bytes=48 << 20
        ),
        name="layer",
    )(tokens, wq, wk, wv, wo, down, up, cosine, sine)


def rotary_tables():
    c = lax.axis_index("ctx")
    base = lax.div(c, 4) * 1024 + lax.rem(c, 2) * 256
    rows = jnp.arange(512, dtype=jnp.int32)
    positions = base + (rows // 256) * 512 + rows % 256
    inverse_freq = 10000.0 ** (-(jnp.arange(HEAD // 2, dtype=F32) * 2.0) / HEAD)
    angles = positions.astype(F32)[:, None] * inverse_freq[None, :]
    cosine, sine = jnp.cos(angles), jnp.sin(angles)
    return jnp.concatenate([cosine, cosine], 1), jnp.concatenate([-sine, sine], 1)


def per_device(tokens, wq, wk, wv, wo, down, up):
    cosine, sine = rotary_tables()
    return layer(tokens, wq, wk, wv, wo, down.reshape(24, D), up.reshape(24, 512), cosine, sine)


def solution(mesh):
    placed = P("ctx", "head")
    return jax.shard_map(
        per_device,
        mesh=mesh,
        in_specs=(placed,) * 5 + (P(), P(None, None, "head")),
        out_specs=placed,
        check_vma=False,
    )
```

```python
import functools

import jax
import jax.numpy as jnp
import numpy as np
from jax import lax
from jax.experimental import pallas as pl
from jax.experimental.pallas import tpu as pltpu
from jax.sharding import PartitionSpec as P

D = 4096
HEADS = 32
HEAD = 128
TOK = 256
MESH = pl.DeviceIdType.MESH
BF16 = jnp.bfloat16
F32 = jnp.float32


class Place:
    def __init__(self):
        c = lax.axis_index("ctx")
        h = lax.axis_index("head")
        self.z = lax.div(c, 4)
        self.xl = lax.rem(lax.div(c, 2), 2)
        self.k = lax.rem(c, 2)
        self.xh = lax.div(h, 4)
        self.y = lax.rem(h, 4)
        self.x = self.xh * 2 + self.xl
        self.h = h
        self.sigma = 1 - 2 * self.k

    def at(self, z=None, x=None, y=None, k=None):
        z = self.z if z is None else z
        x = self.x if x is None else x
        y = self.y if y is None else y
        k = self.k if k is None else k
        return (z * 4 + lax.rem(x, 2) * 2 + k, lax.div(x, 2) * 4 + y)

    def to_z(self, step):
        return self.at(z=lax.rem(self.z + 8 + step, 8))

    def to_x(self, step):
        return self.at(x=lax.rem(self.x + 4 + step, 4))

    def to_y(self, step):
        return self.at(y=lax.rem(self.y + 4 + step, 4))

    def sibling(self):
        return self.at(k=1 - self.k)

    def partner(self):
        return self.at(x=self.xh * 2 + 1 - self.xl)


def greet(devices):
    barrier = pltpu.get_barrier_semaphore()
    for device in devices:
        pl.semaphore_signal(barrier, inc=1, device_id=device, device_id_type=MESH)
    pl.semaphore_wait(barrier, len(devices))


class Sends:
    def __init__(self, send_sem, recv_sem):
        self.send_sem, self.recv_sem, self.count, self.open = send_sem, recv_sem, 0, []

    def slot(self):
        self.count += 1
        return self.count - 1

    def start(self, src, dst, device, slot):
        copy = pltpu.make_async_remote_copy(
            src_ref=src,
            dst_ref=dst,
            send_sem=self.send_sem.at[slot],
            recv_sem=self.recv_sem.at[slot],
            device_id=device,
            device_id_type=MESH,
        )
        copy.start()
        self.open.append(copy)
        return copy

    def finish(self):
        for copy in self.open:
            copy.wait_send()


class Ring4:
    def __init__(self, sends, me, sigma, to, block):
        self.sends, self.me, self.sigma, self.to, self.block = sends, me, sigma, to, block

    def place(self, step):
        return self.block(lax.rem(self.me + 4 + step * self.sigma, 4))

    def start(self):
        own = self.place(0)
        self.ahead = self.sends.start(own, own, self.to(self.sigma), self.sends.slot())
        self.back = self.sends.start(own, own, self.to(-self.sigma), self.sends.slot())

    def forward(self):
        self.ahead.wait_recv()
        block = self.place(-1)
        self.far = self.sends.start(block, block, self.to(self.sigma), self.sends.slot())

    def wait_back(self):
        self.back.wait_recv()

    def wait_far(self):
        self.far.wait_recv()


class PlaneGather:
    def __init__(self, sends, me, block):
        self.me, self.sends = me, sends
        s = me.sigma
        self.first = [
            Ring4(sends, me.x, s, me.to_x, lambda a: block(0, a, me.y)),
            Ring4(sends, me.y, s, me.to_y, lambda a: block(1, me.x, a)),
        ]
        self.second = [[], []]
        for step in (0, -1, 1, -2):
            x = lax.rem(me.x + 4 + step * s, 4)
            y = lax.rem(me.y + 4 + step * s, 4)
            self.second[0].append(Ring4(sends, me.y, s, me.to_y, lambda a, x=x: block(0, x, a)))
            self.second[1].append(Ring4(sends, me.x, s, me.to_x, lambda a, y=y: block(1, a, y)))

    def events(self):
        def start():
            for half in (0, 1):
                self.first[half].start()
            for half in (0, 1):
                self.second[half][0].start()

        def ahead():
            for half in (0, 1):
                self.first[half].forward()
                self.second[half][1].start()

        def back():
            for half in (0, 1):
                self.first[half].wait_back()
                self.second[half][2].start()

        def far():
            for half in (0, 1):
                self.first[half].wait_far()
                self.second[half][3].start()

        def second(i):
            def step():
                for half in (0, 1):
                    self.second[half][i].forward()

            return step

        def finish():
            for half in (0, 1):
                for ring in self.second[half]:
                    ring.wait_back()
                    ring.wait_far()

        return [start, ahead, back, second(0), far, second(1), second(2), second(3), finish]


class HeadGather:
    def __init__(self, sends, me, block):
        self.me, self.sends, self.block = me, sends, block
        far = 1 - me.xh
        self.own_a = Ring4(sends, me.y, me.sigma, me.to_y, lambda a: block(0, me.xh, a))
        self.far_a = Ring4(sends, me.y, me.sigma, me.to_y, lambda a: block(0, far, a))
        self.own_b = Ring4(sends, me.y, me.sigma, me.to_y, lambda a: block(1, me.xh, a))
        self.crossed = []

    def cross(self, half, step):
        block = self.block(half, self.me.xh, lax.rem(self.me.y + 4 + step * self.me.sigma, 4))
        self.crossed.append(
            self.sends.start(block, block, self.me.to_x(2), self.sends.slot())
        )

    def start(self):
        self.cross(0, 0)
        self.own_b.start()
        self.cross(1, 0)
        self.own_a.start()

    def step_1(self):
        self.own_b.forward()
        self.cross(1, -1)
        self.own_b.wait_back()
        self.cross(1, 1)

    def step_2(self):
        self.crossed[0].wait_recv()
        self.far_a.start()
        self.own_a.forward()

    def step_3(self):
        self.own_b.wait_far()
        self.cross(1, -2)
        self.far_a.forward()

    def finish(self):
        for ring in (self.own_a, self.far_a):
            ring.wait_back()
            ring.wait_far()
        for copy in self.crossed[1:]:
            copy.wait_recv()


class RingZ:
    def __init__(self, sends, me, block):
        self.sends, self.me, self.block = sends, me, block
        self.ahead, self.back, self.shared = {}, {}, {}

    def place(self, step, k):
        return self.block(lax.rem(self.me.z + 8 + step, 8), k)

    def share(self, key, step):
        block = self.place(step, self.me.k)
        self.shared[key] = self.sends.start(block, block, self.me.sibling(), self.sends.slot())

    def start(self):
        me, own = self.me, self.place(0, self.me.k)
        self.ahead[1] = self.sends.start(own, own, me.to_z(me.sigma), self.sends.slot())
        self.back[1] = self.sends.start(own, own, me.to_z(-me.sigma), self.sends.slot())
        self.share("own", 0)

    def take_ahead(self, s):
        me = self.me
        self.ahead[s].wait_recv()
        if s < 4:
            block = self.place(-s * me.sigma, me.k)
            self.ahead[s + 1] = self.sends.start(block, block, me.to_z(me.sigma), self.sends.slot())
        self.share(("a", s), -s * me.sigma)

    def take_back(self, s):
        me = self.me
        self.back[s].wait_recv()
        if s < 3:
            block = self.place(s * me.sigma, me.k)
            self.back[s + 1] = self.sends.start(block, block, me.to_z(-me.sigma), self.sends.slot())
        self.share(("b", s), s * me.sigma)

    def wait_shared(self, key):
        self.shared[key].wait_recv()


def layer_kernel(
    tok_in, wq_in, wk_in, wv_in, wo_in, down_in, up_in, angle_in, out_ref,
    down_ref, up_ref, angles, turn, tok, weights, acc, low, qkv, query, kv, total, top, denom, heads_out, merged, wo,
    send_sem, recv_sem, pair_send, pair_recv, hand_send, hand_recv, local_sem,
):
    me = Place()
    w_in = (wq_in, wk_in, wv_in)
    own_cols = pl.multiple_of(me.xl * 256, 256)
    other_cols = pl.multiple_of((1 - me.xl) * 256, 256)
    p = lax.rem(me.z + 8 - 2 * me.xh, 4)
    mine = lax.div(p, 2)
    last = lax.rem(p, 2)

    def plane(q, x=None):
        return me.at(z=lax.rem(me.z + 8 - p + q, 8), x=x)

    partner_x = me.xh * 2 + 1 - me.xl
    local = [pltpu.make_async_copy(tok_in, tok.at[me.h, me.xl], local_sem.at[0])]
    for j in range(3):
        local.append(
            pltpu.make_async_copy(
                w_in[j].at[:, pl.ds(own_cols, 256)], weights.at[j, me.z, me.xl, me.k], local_sem.at[1 + j]
            )
        )
    local.append(pltpu.make_async_copy(wo_in, wo.at[me.z, me.xl, me.k], local_sem.at[4]))
    local.append(pltpu.make_async_copy(down_in, down_ref, local_sem.at[5]))
    local.append(pltpu.make_async_copy(up_in, up_ref, local_sem.at[6]))
    local.append(pltpu.make_async_copy(angle_in, angles, local_sem.at[7]))
    for copy in local:
        copy.start()
    greet(
        [
            me.to_z(1), me.to_z(-1), me.to_x(1), me.to_x(-1), me.to_x(2), me.to_y(1), me.to_y(-1), me.sibling(),
            plane(lax.rem(p + 1, 4)), plane(lax.rem(p + 2, 4)), plane(lax.rem(p + 3, 4)),
            plane(lax.rem(p + 1, 4), partner_x), plane(lax.rem(p + 2, 4), partner_x), plane(lax.rem(p + 3, 4), partner_x),
        ]
    )
    sends = Sends(send_sem, recv_sem)
    trade = []
    for j in range(3):
        trade.append(
            sends.start(
                w_in[j].at[:, pl.ds(other_cols, 256)],
                weights.at[j, me.z, me.xl, me.k],
                me.partner(),
                sends.slot(),
            )
        )
    for copy in local[1:]:
        copy.wait()
    own_ring = RingZ(sends, me, lambda z, k: weights.at[:, z, me.xl, k])
    other_ring = RingZ(sends, me, lambda z, k: weights.at[:, z, 1 - me.xl, k])
    own_ring.start()
    local[0].wait()

    def block(half, x, y):
        return tok.at[lax.div(x, 2) * 4 + y, lax.rem(x, 2), pl.ds(half * 128, 128)]

    events = PlaneGather(sends, me, block).events()
    events[0]()
    events[1]()
    for copy in trade:
        copy.wait_recv()
    other_ring.start()
    own_ring.take_ahead(1)
    own_ring.take_back(1)
    events[2]()
    events[3]()
    events[4]()
    other_ring.take_ahead(1)
    other_ring.take_back(1)
    events[5]()
    events[6]()
    own_ring.take_ahead(2)
    own_ring.take_back(2)
    events[7]()
    other_ring.take_ahead(2)
    other_ring.take_back(2)
    events[8]()
    own_ring.take_ahead(3)
    own_ring.take_back(3)
    trade_wo = sends.start(
        wo.at[me.z, me.xl, me.k], wo.at[me.z, me.xl, me.k], me.partner(), sends.slot()
    )

    def multiply(step, first=False):
        chunk = lax.rem(me.z + 8 + step, 8)
        left = tok[chunk].reshape(512, 512)
        for j in (1, 2, 0):
            part = jnp.dot(left, weights[j, chunk].reshape(512, 256), preferred_element_type=F32)
            if first:
                acc[j] = part
            else:
                acc[j] += part

    for half in range(2):
        block_row = 256 + me.z * 4 + half * 2 + me.k
        block_cos, block_sin = angles[0, pl.ds(block_row, 1)], angles[1, pl.ds(block_row, 1)]
        row_cos, row_sin = angles[0, pl.ds(0, TOK)], angles[1, pl.ds(0, TOK)]
        turn[0, pl.ds(half * TOK, TOK)] = row_cos * block_cos - row_sin * block_sin
        lane = lax.broadcasted_iota(jnp.int32, (TOK, HEAD), 1)
        sine = row_sin * block_cos + row_cos * block_sin
        turn[1, pl.ds(half * TOK, TOK)] = jnp.where(lane < HEAD // 2, -sine, sine)

    def low_rank(chunk, so_far):
        left = tok[chunk].reshape(512, 512)
        cols = pl.multiple_of(chunk * 512, 512)
        return so_far + lax.dot_general(
            left, down_ref[:, pl.ds(cols, 512)], (((1,), (1,)), ((), ())), preferred_element_type=F32
        )

    def shared(key):
        own_ring.wait_shared(key)
        other_ring.wait_shared(key)

    shared("own")
    multiply(0, True)
    low[...] = lax.fori_loop(0, 4, low_rank, jnp.zeros((512, 24), F32))
    shared(("a", 1))
    shared(("b", 1))
    multiply(1)
    multiply(-1)
    other_ring.take_ahead(3)
    other_ring.take_back(3)
    shared(("a", 2))
    shared(("b", 2))
    multiply(2)
    multiply(-2)
    rank = lax.fori_loop(4, 8, low_rank, low[...]).astype(BF16)
    rank_of = lax.broadcasted_iota(jnp.int32, (512, 24), 1) // 8
    for j in range(3):
        part_rank = jnp.where(rank_of == j, rank, jnp.zeros_like(rank))
        acc[j] += 2.0 * jnp.dot(
            part_rank, up_ref[:, pl.ds(own_cols, 256)], preferred_element_type=F32
        )
    own_ring.take_ahead(4)
    shared(("a", 3))
    shared(("b", 3))
    multiply(3)
    multiply(-3)
    top[...] = jnp.full_like(top, -1e30)
    denom[...] = jnp.zeros_like(denom)
    total[...] = jnp.zeros_like(total)
    other_ring.take_ahead(4)
    shared(("a", 4))
    multiply(4)

    def finish_projection(j):
        for head in range(2):
            part = acc[j, :, head * HEAD : (head + 1) * HEAD]
            if j < 2:
                part = part * turn[0] + pltpu.roll(part, HEAD // 2, 1) * turn[1]
            qkv[head, j] = part.astype(BF16)

    def kv_copy(src, b, device, send):
        return pltpu.make_async_remote_copy(
            src, kv.at[b, me.k], pair_send.at[send], pair_recv.at[b],
            device_id=device, device_id_type=MESH,
        )

    def q_copy(head, b, device, send):
        return pltpu.make_async_remote_copy(
            qkv.at[head, 0], query.at[b], pair_send.at[send], pair_recv.at[4 + b],
            device_id=device, device_id_type=MESH,
        )

    def kv_of(head):
        return qkv.at[head, pl.ds(1, 2)]

    def share(b, src):
        return pltpu.make_async_remote_copy(
            src, kv.at[b, me.k], pair_send.at[8 + b], pair_recv.at[8 + b],
            device_id=me.sibling(), device_id_type=MESH,
        )

    finish_projection(1)
    finish_projection(2)

    @pl.when(p == 0)
    def _():
        kv_copy(kv_of(0), 0, plane(1), 1).start()

    @pl.when(p == 1)
    def _():
        kv_copy(kv_of(1), 1, plane(2), 1).start()

    @pl.when(p == 2)
    def _():
        kv_copy(kv_of(0), 2, plane(1), 0).start()
        kv_copy(kv_of(1), 2, plane(3), 1).start()

    share(p, kv_of(mine)).start()
    finish_projection(0)

    @pl.when(p == 1)
    def _():
        q_copy(0, 1, plane(0), 2).start()
        kv_copy(kv_of(0), 1, plane(0), 0).start()

    @pl.when(p != 1)
    def _():
        query[p] = qkv[mine, 0]

    kv[p, me.k] = qkv[mine, 1:3]
    ring_a = RingZ(sends, me, lambda z, k: wo.at[z, me.xl, k])
    ring_b = RingZ(sends, me, lambda z, k: wo.at[z, 1 - me.xl, k])
    scale = HEAD ** (-0.5)

    def allowed(half, core, keys):
        rows = lax.broadcasted_iota(jnp.int32, (TOK, keys), 0)
        cols = lax.broadcasted_iota(jnp.int32, (TOK, keys), 1)
        place = cols + jnp.where(cols >= TOK, 256, 0)
        return place + core * 256 <= rows + half * 512 + me.k * 256

    def pair(slot, b, diagonal):
        for half in range(2):
            part = pl.ds(half * TOK, TOK)
            keys = TOK if diagonal and half == 0 else 2 * TOK
            q = query[slot, part]
            scores = []
            for core in range(2):
                score = lax.dot_general(
                    q, kv[b, core, 0, pl.ds(0, keys)], (((1,), (1,)), ((), ())), preferred_element_type=F32
                ) * scale
                if diagonal:
                    score = jnp.where(allowed(half, core, keys), score, -1e30)
                scores.append(score)
            old = top[slot, part]
            new = jnp.maximum(old, jnp.max(jnp.maximum(scores[0], scores[1]), axis=1, keepdims=True))
            probs = [jnp.exp(score - new) for score in scores]
            if diagonal:
                probs = [
                    jnp.where(allowed(half, core, keys), probs[core], 0.0) for core in range(2)
                ]
            factor = jnp.exp(old - new)
            top[slot, part] = new
            denom[slot, part] = denom[slot, part] * factor + jnp.sum(
                probs[0] + probs[1], axis=1, keepdims=True
            )
            result = total[slot, part] * factor
            for core in range(2):
                result = result + jnp.dot(
                    probs[core].astype(BF16),
                    kv[b, core, 1, pl.ds(0, keys)],
                    preferred_element_type=F32,
                )
            total[slot, part] = result

    def rows_of(r):
        return pl.ds(pl.multiple_of(r * TOK, TOK), TOK)

    place = merged.at[me.h, me.xl * 2 + mine]

    def hand_copy(b, r, x, column):
        return pltpu.make_async_remote_copy(
            heads_out.at[b, rows_of(r)], place, hand_send.at[2 * b + column], hand_recv.at[2 * mine + column],
            device_id=plane(b, x), device_id_type=MESH,
        )

    def hand_over(b):
        heads_out[b] = (total[b] / denom[b]).astype(BF16)
        hand_copy(b, 1 - me.xl, partner_x, 1).start()

        @pl.when(b != p)
        def _():
            hand_copy(b, me.xl, me.x, 0).start()

        @pl.when(b == p)
        def _():
            merged[me.h, me.xl * 2 + mine] = heads_out[p, rows_of(me.xl)]

    def arrive(b, onward=None):
        kv_copy(kv.at[b, me.k], b, me.sibling(), 0).wait_recv()
        if onward is not None:
            kv_copy(kv.at[b, me.k], b, plane(onward), 4 + b).start()
        share(b, kv.at[b, me.k]).start()

    def got_query(b):
        q_copy(0, b, me.sibling(), 2).wait_recv()

    def whole(b):
        share(b, kv.at[b, me.k]).wait_recv()

    def pairs(first, count, b):
        def one(i, c):
            pair(first + i, b, False)
            return c

        lax.fori_loop(0, count, one, 0)

    whole(p)

    @pl.when(p != 1)
    def _():
        pair(p, p, True)

    one = 1 + last

    @pl.when(p == 0)
    def _():
        kv_copy(kv_of(0), 0, me.sibling(), 1).wait_send()
        kv_copy(kv_of(1), 0, plane(2), 0).start()
        arrive(1)
        got_query(1)

    @pl.when(p == 1)
    def _():
        arrive(2, 0)
        got_query(3)
        q_copy(1, 1, plane(2), 3).start()

    @pl.when(p == 2)
    def _():
        arrive(1, 3)
        kv_copy(kv_of(0), 2, me.sibling(), 0).wait_send()
        q_copy(0, 2, plane(0), 2).start()

    @pl.when(p == 3)
    def _():
        arrive(2)
        q_copy(0, 3, plane(1), 2).start()
        kv_copy(kv_of(0), 3, plane(1), 0).start()

    whole(one)

    @pl.when(p == 0)
    def _():
        pair(1, 1, True)

    def second(i, c):
        q = jnp.where(p == 0, 1, jnp.where(p == 2, 2, 3))
        b = jnp.where(p == 0, 0, jnp.where(p == 1, 1 + i, jnp.where(p == 2, 1, 2)))
        pair(q, b, False)
        return c

    lax.fori_loop(0, jnp.where(p == 1, 2, 1), second, 0)

    @pl.when(p == 0)
    def _():
        hand_over(1)
        hand_over(0)
        kv_copy(kv_of(1), 0, me.sibling(), 0).wait_send()
        q_copy(1, 0, plane(2), 2).start()
        got_query(2)

    @pl.when(p == 1)
    def _():
        arrive(0)

    @pl.when(p == 2)
    def _():
        arrive(0, 3)
        got_query(1)

    @pl.when(p == 3)
    def _():
        arrive(1)

    @pl.when(p != 0)
    def _():
        whole(jnp.where(p == 3, 1, 0))

    trade_wo.wait_recv()
    ring_a.start()
    def third(i, c):
        q = jnp.where(p == 0, 2, jnp.where(p == 2, 1 + i, 3))
        b = jnp.where(p == 0, i, jnp.where(p == 3, 1, 0))
        pair(q, b, False)
        return c

    lax.fori_loop(0, 2 - last, third, 0)

    @pl.when(p == 0)
    def _():
        arrive(2)
        whole(2)

    @pl.when(p == 1)
    def _():
        arrive(3)
        whole(3)

    @pl.when(p == 2)
    def _():
        hand_over(2)
        pair(1, 1, True)
        hand_over(1)
        got_query(0)

    @pl.when(p != 3)
    def _():
        q = jnp.where(p == 0, 2, jnp.where(p == 1, 3, 0))
        pair(q, q, True)

    @pl.when(p == 3)
    def _():
        arrive(0)
        whole(0)
        pair(3, 0, False)

    @pl.when(p == 0)
    def _():
        hand_over(2)

    @pl.when(p == 2)
    def _():
        hand_over(0)

    @pl.when(last == 1)
    def _():
        hand_over(3)

    ring_b.start()
    for head in range(2):
        pltpu.make_async_remote_copy(
            heads_out.at[0, pl.ds(0, TOK)], place, hand_send.at[0], hand_recv.at[2 * head + 1],
            device_id=me.sibling(), device_id_type=MESH,
        ).wait_recv()
        here = (p == 0) if head == 0 else (p >= 2)

        @pl.when(jnp.logical_not(here))
        def _():
            pltpu.make_async_remote_copy(
                heads_out.at[0, pl.ds(0, TOK)], place, hand_send.at[0], hand_recv.at[2 * head],
                device_id=me.sibling(), device_id_type=MESH,
            ).wait_recv()

    gather = HeadGather(sends, me, lambda half, xh, y: merged.at[xh * 4 + y, pl.ds(half * 2, 2)])
    gather.start()
    ring_a.take_ahead(1)
    ring_a.take_back(1)
    ring_b.take_ahead(1)
    ring_b.take_back(1)
    gather.step_1()
    gather.step_2()
    ring_a.take_ahead(2)
    ring_a.take_back(2)
    ring_b.take_ahead(2)
    ring_b.take_back(2)
    gather.step_3()
    ring_a.take_ahead(3)
    ring_a.take_back(3)
    ring_b.take_ahead(3)
    ring_b.take_back(3)
    gather.finish()

    def merge(step, so_far):
        h = lax.rem(me.z + 8 + step, 8)
        for half in range(2):
            left = jnp.concatenate([merged[h, 2 * half], merged[h, 2 * half + 1]], axis=1)
            so_far = so_far + jnp.dot(
                left, wo[h, half].reshape(256, 512), preferred_element_type=F32
            )
        return so_far

    def ready(key):
        ring_a.wait_shared(key)
        ring_b.wait_shared(key)

    ready("own")
    result = merge(0, jnp.zeros((TOK, 512), F32))
    for s in (1, 2):
        ready(("a", s))
        ready(("b", s))
        result = merge(-s, merge(s, result))
    ring_a.take_ahead(4)
    ready(("a", 3))
    ready(("b", 3))
    result = merge(-3, merge(3, result))
    ring_b.take_ahead(4)
    ready(("a", 4))
    out_ref[...] = merge(4, result).astype(BF16)

    q_copy(0, 0, me.sibling(), 2).wait_send()

    @pl.when(last == 1)
    def _():
        kv_copy(kv_of(0), 0, me.sibling(), 0).wait_send()

    @pl.when((p == 1) | (p == 2))
    def _():
        kv_copy(kv_of(0), 0, me.sibling(), 1).wait_send()

    @pl.when(p == 1)
    def _():
        q_copy(0, 0, me.sibling(), 3).wait_send()
        kv_copy(kv_of(0), 0, me.sibling(), 6).wait_send()

    @pl.when(p == 2)
    def _():
        kv_copy(kv_of(0), 0, me.sibling(), 4).wait_send()
        kv_copy(kv_of(0), 0, me.sibling(), 5).wait_send()

    for b in range(3):
        share(b, kv_of(0)).wait_send()

    @pl.when(last == 1)
    def _():
        share(3, kv_of(0)).wait_send()
        hand_copy(3, 0, partner_x, 1).wait_send()

    @pl.when(p == 1)
    def _():
        hand_copy(3, 0, me.x, 0).wait_send()

    @pl.when(last == 0)
    def _():
        for b in range(3):
            hand_copy(b, 0, partner_x, 1).wait_send()

            @pl.when(b != p)
            def _():
                hand_copy(b, 0, me.x, 0).wait_send()

    sends.finish()


def layer(tokens, wq, wk, wv, wo, down, up, angles):
    slots = 120
    any_spec = pl.BlockSpec(memory_space=pl.ANY)
    vmem = pl.BlockSpec(memory_space=pltpu.VMEM)
    return pl.pallas_call(
        layer_kernel,
        out_shape=jax.ShapeDtypeStruct((TOK, 512), BF16),
        in_specs=[any_spec] * 8,
        out_specs=vmem,
        scratch_shapes=[
            pltpu.VMEM((24, D), BF16),
            pltpu.VMEM((24, 512), BF16),
            pltpu.VMEM((2, 288, HEAD), F32),
            pltpu.VMEM((2, 512, HEAD), F32),
            pltpu.VMEM((8, 2, TOK, 512), BF16),
            pltpu.VMEM((3, 8, 2, 2, 128, 256), BF16),
            pltpu.VMEM((3, 512, 256), F32),
            pltpu.VMEM((512, 24), F32),
            pltpu.VMEM((2, 3, 512, HEAD), BF16),
            pltpu.VMEM((4, 512, HEAD), BF16),
            pltpu.VMEM((4, 2, 2, 512, HEAD), BF16),
            pltpu.VMEM((4, 512, HEAD), F32),
            pltpu.VMEM((4, 512, 1), F32),
            pltpu.VMEM((4, 512, 1), F32),
            pltpu.VMEM((4, 512, HEAD), BF16),
            pltpu.VMEM((8, 4, TOK, HEAD), BF16),
            pltpu.VMEM((8, 2, 2, 128, 512), BF16),
            pltpu.SemaphoreType.DMA((slots,)),
            pltpu.SemaphoreType.DMA((slots,)),
            pltpu.SemaphoreType.DMA((12,)),
            pltpu.SemaphoreType.DMA((12,)),
            pltpu.SemaphoreType.DMA((8,)),
            pltpu.SemaphoreType.DMA((4,)),
            pltpu.SemaphoreType.DMA((8,)),
        ],
        compiler_params=pltpu.CompilerParams(
            collective_id=0, has_side_effects=True, vmem_limit_bytes=60 << 20
        ),
        name="layer",
    )(tokens, wq, wk, wv, wo, down, up, angles)


def rotary_tables():
    rows = np.concatenate([np.arange(TOK), np.arange(32) * TOK]).astype(np.float64)
    inverse_freq = 10000.0 ** (-(np.arange(HEAD // 2) * 2.0) / HEAD)
    angle = rows[:, None] * np.concatenate([inverse_freq, inverse_freq])[None, :]
    return np.stack([np.cos(angle), np.sin(angle)]).astype(np.float32)


def per_device(tokens, wq, wk, wv, wo, down, up):
    return layer(tokens, wq, wk, wv, wo, down.reshape(24, D), up.reshape(24, 512), jnp.asarray(rotary_tables()))


def solution(mesh):
    placed = P("ctx", "head")
    return jax.shard_map(
        per_device,
        mesh=mesh,
        in_specs=(placed,) * 5 + (P(), P(None, None, "head")),
        out_specs=placed,
        check_vma=False,
    )
```

```python
import functools

import jax
import jax.numpy as jnp
import numpy as np
from jax import lax
from jax.experimental import pallas as pl
from jax.experimental.pallas import tpu as pltpu
from jax.sharding import PartitionSpec as P

D = 4096
HEADS = 32
HEAD = 128
TOK = 256
MESH = pl.DeviceIdType.MESH
BF16 = jnp.bfloat16
F32 = jnp.float32


class Place:
    def __init__(self):
        c = lax.axis_index("ctx")
        h = lax.axis_index("head")
        self.z = lax.div(c, 4)
        self.xl = lax.rem(lax.div(c, 2), 2)
        self.k = lax.rem(c, 2)
        self.xh = lax.div(h, 4)
        self.y = lax.rem(h, 4)
        self.x = self.xh * 2 + self.xl
        self.h = h
        self.sigma = 1 - 2 * self.k

    def at(self, z=None, x=None, y=None, k=None):
        z = self.z if z is None else z
        x = self.x if x is None else x
        y = self.y if y is None else y
        k = self.k if k is None else k
        return (z * 4 + lax.rem(x, 2) * 2 + k, lax.div(x, 2) * 4 + y)

    def to_z(self, step):
        return self.at(z=lax.rem(self.z + 8 + step, 8))

    def to_x(self, step):
        return self.at(x=lax.rem(self.x + 4 + step, 4))

    def to_y(self, step):
        return self.at(y=lax.rem(self.y + 4 + step, 4))

    def sibling(self):
        return self.at(k=1 - self.k)

    def partner(self):
        return self.at(x=self.xh * 2 + 1 - self.xl)


def greet(devices):
    barrier = pltpu.get_barrier_semaphore()
    for device in devices:
        pl.semaphore_signal(barrier, inc=1, device_id=device, device_id_type=MESH)
    pl.semaphore_wait(barrier, len(devices))


class Sends:
    def __init__(self, send_sem, recv_sem):
        self.send_sem, self.recv_sem, self.count, self.open = send_sem, recv_sem, 0, []

    def slot(self):
        self.count += 1
        return self.count - 1

    def start(self, src, dst, device, slot):
        copy = pltpu.make_async_remote_copy(
            src_ref=src,
            dst_ref=dst,
            send_sem=self.send_sem.at[slot],
            recv_sem=self.recv_sem.at[slot],
            device_id=device,
            device_id_type=MESH,
        )
        copy.start()
        self.open.append(copy)
        return copy

    def finish(self):
        for copy in self.open:
            copy.wait_send()


class Ring4:
    def __init__(self, sends, me, sigma, to, block):
        self.sends, self.me, self.sigma, self.to, self.block = sends, me, sigma, to, block

    def place(self, step):
        return self.block(lax.rem(self.me + 4 + step * self.sigma, 4))

    def start(self):
        own = self.place(0)
        self.ahead = self.sends.start(own, own, self.to(self.sigma), self.sends.slot())
        self.back = self.sends.start(own, own, self.to(-self.sigma), self.sends.slot())

    def forward(self):
        self.ahead.wait_recv()
        block = self.place(-1)
        self.far = self.sends.start(block, block, self.to(self.sigma), self.sends.slot())

    def wait_back(self):
        self.back.wait_recv()

    def wait_far(self):
        self.far.wait_recv()


class PlaneGather:
    def __init__(self, sends, me, block):
        self.me, self.sends = me, sends
        s = me.sigma
        self.first = [
            Ring4(sends, me.x, s, me.to_x, lambda a: block(0, a, me.y)),
            Ring4(sends, me.y, s, me.to_y, lambda a: block(1, me.x, a)),
        ]
        self.second = [[], []]
        for step in (0, -1, 1, -2):
            x = lax.rem(me.x + 4 + step * s, 4)
            y = lax.rem(me.y + 4 + step * s, 4)
            self.second[0].append(Ring4(sends, me.y, s, me.to_y, lambda a, x=x: block(0, x, a)))
            self.second[1].append(Ring4(sends, me.x, s, me.to_x, lambda a, y=y: block(1, a, y)))

    def events(self):
        def start():
            for half in (0, 1):
                self.first[half].start()
            for half in (0, 1):
                self.second[half][0].start()

        def ahead():
            for half in (0, 1):
                self.first[half].forward()
                self.second[half][1].start()

        def back():
            for half in (0, 1):
                self.first[half].wait_back()
                self.second[half][2].start()

        def far():
            for half in (0, 1):
                self.first[half].wait_far()
                self.second[half][3].start()

        def second(i):
            def step():
                for half in (0, 1):
                    self.second[half][i].forward()

            return step

        def finish():
            for half in (0, 1):
                for ring in self.second[half]:
                    ring.wait_back()
                    ring.wait_far()

        return [start, ahead, back, second(0), far, second(1), second(2), second(3), finish]


class HeadGather:
    def __init__(self, sends, me, block):
        self.me, self.sends, self.block = me, sends, block
        far = 1 - me.xh
        self.own_a = Ring4(sends, me.y, me.sigma, me.to_y, lambda a: block(0, me.xh, a))
        self.far_a = Ring4(sends, me.y, me.sigma, me.to_y, lambda a: block(0, far, a))
        self.own_b = Ring4(sends, me.y, me.sigma, me.to_y, lambda a: block(1, me.xh, a))
        self.crossed = []

    def cross(self, half, step):
        block = self.block(half, self.me.xh, lax.rem(self.me.y + 4 + step * self.me.sigma, 4))
        self.crossed.append(
            self.sends.start(block, block, self.me.to_x(2), self.sends.slot())
        )

    def start_a(self):
        self.cross(0, 0)
        self.own_a.start()

    def start_b(self):
        self.own_b.start()
        self.cross(1, 0)

    def step_1(self):
        self.own_b.forward()
        self.cross(1, -1)
        self.own_b.wait_back()
        self.cross(1, 1)

    def step_2(self):
        self.crossed[0].wait_recv()
        self.far_a.start()
        self.own_a.forward()

    def step_3(self):
        self.own_b.wait_far()
        self.cross(1, -2)
        self.far_a.forward()

    def finish(self):
        for ring in (self.own_a, self.far_a):
            ring.wait_back()
            ring.wait_far()
        for copy in self.crossed[1:]:
            copy.wait_recv()


class RingZ:
    def __init__(self, sends, me, block):
        self.sends, self.me, self.block = sends, me, block
        self.ahead, self.back, self.shared = {}, {}, {}

    def place(self, step, k):
        return self.block(lax.rem(self.me.z + 8 + step, 8), k)

    def share(self, key, step):
        block = self.place(step, self.me.k)
        self.shared[key] = self.sends.start(block, block, self.me.sibling(), self.sends.slot())

    def start(self):
        me, own = self.me, self.place(0, self.me.k)
        self.ahead[1] = self.sends.start(own, own, me.to_z(me.sigma), self.sends.slot())
        self.back[1] = self.sends.start(own, own, me.to_z(-me.sigma), self.sends.slot())
        self.share("own", 0)

    def take_ahead(self, s):
        me = self.me
        self.ahead[s].wait_recv()
        if s < 4:
            block = self.place(-s * me.sigma, me.k)
            self.ahead[s + 1] = self.sends.start(block, block, me.to_z(me.sigma), self.sends.slot())
        self.share(("a", s), -s * me.sigma)

    def take_back(self, s):
        me = self.me
        self.back[s].wait_recv()
        if s < 3:
            block = self.place(s * me.sigma, me.k)
            self.back[s + 1] = self.sends.start(block, block, me.to_z(-me.sigma), self.sends.slot())
        self.share(("b", s), s * me.sigma)

    def wait_shared(self, key):
        self.shared[key].wait_recv()


def layer_kernel(
    tok_in, wq_in, wk_in, wv_in, wo_in, down_in, up_in, angle_in, out_ref,
    down_ref, up_ref, angles, turn, tok, weights, acc, low, qkv, query, kv, total, top, denom, heads_out, merged, wo,
    send_sem, recv_sem, pair_send, pair_recv, hand_send, hand_recv, local_sem,
):
    me = Place()
    w_in = (wq_in, wk_in, wv_in)
    own_cols = pl.multiple_of(me.xl * 256, 256)
    other_cols = pl.multiple_of((1 - me.xl) * 256, 256)
    p = lax.rem(me.z + 8 - 2 * me.xh, 4)
    mine = lax.div(p, 2)
    last = lax.rem(p, 2)

    def plane(q, x=None):
        return me.at(z=lax.rem(me.z + 8 - p + q, 8), x=x)

    partner_x = me.xh * 2 + 1 - me.xl
    local = [pltpu.make_async_copy(tok_in, tok.at[me.h, me.xl], local_sem.at[0])]
    for j in range(3):
        local.append(
            pltpu.make_async_copy(
                w_in[j].at[:, pl.ds(own_cols, 256)], weights.at[j, me.z, me.xl, me.k], local_sem.at[1 + j]
            )
        )
    local.append(pltpu.make_async_copy(wo_in, wo.at[me.z, me.xl, me.k], local_sem.at[4]))
    local.append(pltpu.make_async_copy(down_in, down_ref, local_sem.at[5]))
    local.append(pltpu.make_async_copy(up_in, up_ref, local_sem.at[6]))
    local.append(pltpu.make_async_copy(angle_in, angles, local_sem.at[7]))
    for copy in local:
        copy.start()
    greet(
        [
            me.to_z(1), me.to_z(-1), me.to_x(1), me.to_x(-1), me.to_x(2), me.to_y(1), me.to_y(-1), me.sibling(),
            plane(lax.rem(p + 1, 4)), plane(lax.rem(p + 2, 4)), plane(lax.rem(p + 3, 4)),
            plane(lax.rem(p + 1, 4), partner_x), plane(lax.rem(p + 2, 4), partner_x), plane(lax.rem(p + 3, 4), partner_x),
        ]
    )
    sends = Sends(send_sem, recv_sem)
    trade = []
    for j in range(3):
        trade.append(
            sends.start(
                w_in[j].at[:, pl.ds(other_cols, 256)],
                weights.at[j, me.z, me.xl, me.k],
                me.partner(),
                sends.slot(),
            )
        )
    for copy in local[1:]:
        copy.wait()
    own_ring = RingZ(sends, me, lambda z, k: weights.at[:, z, me.xl, k])
    other_ring = RingZ(sends, me, lambda z, k: weights.at[:, z, 1 - me.xl, k])
    own_ring.start()
    local[0].wait()

    def block(half, x, y):
        return tok.at[lax.div(x, 2) * 4 + y, lax.rem(x, 2), pl.ds(half * 128, 128)]

    events = PlaneGather(sends, me, block).events()
    events[0]()
    events[1]()
    for copy in trade:
        copy.wait_recv()
    other_ring.start()
    own_ring.take_ahead(1)
    own_ring.take_back(1)
    events[2]()
    events[3]()
    events[4]()
    other_ring.take_ahead(1)
    other_ring.take_back(1)
    events[5]()
    events[6]()
    own_ring.take_ahead(2)
    own_ring.take_back(2)
    events[7]()
    other_ring.take_ahead(2)
    other_ring.take_back(2)
    events[8]()
    own_ring.take_ahead(3)
    own_ring.take_back(3)
    trade_wo = sends.start(
        wo.at[me.z, me.xl, me.k], wo.at[me.z, me.xl, me.k], me.partner(), sends.slot()
    )

    def multiply(step, first=False):
        chunk = lax.rem(me.z + 8 + step, 8)
        left = tok[chunk].reshape(512, 512)
        for j in (1, 2, 0):
            part = jnp.dot(left, weights[j, chunk].reshape(512, 256), preferred_element_type=F32)
            if first:
                acc[j] = part
            else:
                acc[j] += part

    for half in range(2):
        block_row = 256 + me.z * 4 + half * 2 + me.k
        block_cos, block_sin = angles[0, pl.ds(block_row, 1)], angles[1, pl.ds(block_row, 1)]
        row_cos, row_sin = angles[0, pl.ds(0, TOK)], angles[1, pl.ds(0, TOK)]
        turn[0, pl.ds(half * TOK, TOK)] = row_cos * block_cos - row_sin * block_sin
        lane = lax.broadcasted_iota(jnp.int32, (TOK, HEAD), 1)
        sine = row_sin * block_cos + row_cos * block_sin
        turn[1, pl.ds(half * TOK, TOK)] = jnp.where(lane < HEAD // 2, -sine, sine)

    def low_rank(chunk, so_far):
        left = tok[chunk].reshape(512, 512)
        cols = pl.multiple_of(chunk * 512, 512)
        return so_far + lax.dot_general(
            left, down_ref[:, pl.ds(cols, 512)], (((1,), (1,)), ((), ())), preferred_element_type=F32
        )

    def shared(key):
        own_ring.wait_shared(key)
        other_ring.wait_shared(key)

    shared("own")
    multiply(0, True)
    low[...] = lax.fori_loop(0, 4, low_rank, jnp.zeros((512, 24), F32))
    shared(("a", 1))
    shared(("b", 1))
    multiply(1)
    multiply(-1)
    other_ring.take_ahead(3)
    other_ring.take_back(3)
    shared(("a", 2))
    shared(("b", 2))
    multiply(2)
    multiply(-2)
    rank = lax.fori_loop(4, 8, low_rank, low[...]).astype(BF16)
    rank_of = lax.broadcasted_iota(jnp.int32, (512, 24), 1) // 8
    for j in range(3):
        part_rank = jnp.where(rank_of == j, rank, jnp.zeros_like(rank))
        acc[j] += 2.0 * jnp.dot(
            part_rank, up_ref[:, pl.ds(own_cols, 256)], preferred_element_type=F32
        )
    own_ring.take_ahead(4)
    shared(("a", 3))
    shared(("b", 3))
    multiply(3)
    multiply(-3)
    top[...] = jnp.full_like(top, -1e30)
    denom[...] = jnp.zeros_like(denom)
    total[...] = jnp.zeros_like(total)
    other_ring.take_ahead(4)
    shared(("a", 4))
    multiply(4)

    def finish_projection(j):
        for head in range(2):
            part = acc[j, :, head * HEAD : (head + 1) * HEAD]
            if j < 2:
                part = part * turn[0] + pltpu.roll(part, HEAD // 2, 1) * turn[1]
            qkv[head, j] = part.astype(BF16)

    def kv_copy(src, b, device, send):
        return pltpu.make_async_remote_copy(
            src, kv.at[b, me.k], pair_send.at[send], pair_recv.at[b],
            device_id=device, device_id_type=MESH,
        )

    def q_copy(head, b, device, send):
        return pltpu.make_async_remote_copy(
            qkv.at[head, 0], query.at[b], pair_send.at[send], pair_recv.at[4 + b],
            device_id=device, device_id_type=MESH,
        )

    def kv_of(head):
        return qkv.at[head, pl.ds(1, 2)]

    def share(b, src):
        return pltpu.make_async_remote_copy(
            src, kv.at[b, me.k], pair_send.at[8 + b], pair_recv.at[8 + b],
            device_id=me.sibling(), device_id_type=MESH,
        )

    finish_projection(1)
    finish_projection(2)

    @pl.when(p == 0)
    def _():
        kv_copy(kv_of(0), 0, plane(1), 1).start()

    @pl.when(p == 1)
    def _():
        kv_copy(kv_of(1), 1, plane(2), 1).start()

    @pl.when(p == 2)
    def _():
        kv_copy(kv_of(0), 2, plane(1), 0).start()
        kv_copy(kv_of(1), 2, plane(3), 1).start()

    share(p, kv_of(mine)).start()
    finish_projection(0)

    @pl.when(p == 1)
    def _():
        q_copy(0, 1, plane(0), 2).start()
        kv_copy(kv_of(0), 1, plane(0), 0).start()

    @pl.when(p != 1)
    def _():
        query[p] = qkv[mine, 0]

    kv[p, me.k] = qkv[mine, 1:3]
    ring_a = RingZ(sends, me, lambda z, k: wo.at[z, me.xl, k])
    ring_b = RingZ(sends, me, lambda z, k: wo.at[z, 1 - me.xl, k])
    scale = HEAD ** (-0.5)

    def allowed(half, core, keys):
        rows = lax.broadcasted_iota(jnp.int32, (TOK, keys), 0)
        cols = lax.broadcasted_iota(jnp.int32, (TOK, keys), 1)
        place = cols + jnp.where(cols >= TOK, 256, 0)
        return place + core * 256 <= rows + half * 512 + me.k * 256

    def pair(slot, b, diagonal):
        for half in range(2):
            part = pl.ds(half * TOK, TOK)
            keys = TOK if diagonal and half == 0 else 2 * TOK
            q = query[slot, part]
            scores = []
            for core in range(2):
                score = lax.dot_general(
                    q, kv[b, core, 0, pl.ds(0, keys)], (((1,), (1,)), ((), ())), preferred_element_type=F32
                ) * scale
                if diagonal:
                    score = jnp.where(allowed(half, core, keys), score, -1e30)
                scores.append(score)
            old = top[slot, part]
            new = jnp.maximum(old, jnp.max(jnp.maximum(scores[0], scores[1]), axis=1, keepdims=True))
            probs = [jnp.exp(score - new) for score in scores]
            if diagonal:
                probs = [
                    jnp.where(allowed(half, core, keys), probs[core], 0.0) for core in range(2)
                ]
            factor = jnp.exp(old - new)
            top[slot, part] = new
            denom[slot, part] = denom[slot, part] * factor + jnp.sum(
                probs[0] + probs[1], axis=1, keepdims=True
            )
            result = total[slot, part] * factor
            for core in range(2):
                result = result + jnp.dot(
                    probs[core].astype(BF16),
                    kv[b, core, 1, pl.ds(0, keys)],
                    preferred_element_type=F32,
                )
            total[slot, part] = result

    def rows_of(r):
        return pl.ds(pl.multiple_of(r * TOK, TOK), TOK)

    place = merged.at[me.h, mine, me.xl]

    def hand_copy(b, r, x, column):
        return pltpu.make_async_remote_copy(
            heads_out.at[b, rows_of(r)], place, hand_send.at[2 * b + column], hand_recv.at[2 * mine + column],
            device_id=plane(b, x), device_id_type=MESH,
        )

    def hand_over(b):
        heads_out[b] = (total[b] / denom[b]).astype(BF16)
        hand_copy(b, 1 - me.xl, partner_x, 1).start()

        @pl.when(b != p)
        def _():
            hand_copy(b, me.xl, me.x, 0).start()

        @pl.when(b == p)
        def _():
            merged[me.h, mine, me.xl] = heads_out[p, rows_of(me.xl)]

    def arrive(b, onward=None):
        kv_copy(kv.at[b, me.k], b, me.sibling(), 0).wait_recv()
        if onward is not None:
            kv_copy(kv.at[b, me.k], b, plane(onward), 4 + b).start()
        share(b, kv.at[b, me.k]).start()

    def got_query(b):
        q_copy(0, b, me.sibling(), 2).wait_recv()

    def whole(b):
        share(b, kv.at[b, me.k]).wait_recv()

    def pairs(first, count, b):
        def one(i, c):
            pair(first + i, b, False)
            return c

        lax.fori_loop(0, count, one, 0)

    whole(p)

    @pl.when(p != 1)
    def _():
        pair(p, p, True)

    one = 1 + last

    @pl.when(p == 0)
    def _():
        kv_copy(kv_of(0), 0, me.sibling(), 1).wait_send()
        kv_copy(kv_of(1), 0, plane(2), 0).start()
        arrive(1)
        got_query(1)

    @pl.when(p == 1)
    def _():
        arrive(2, 0)
        got_query(3)
        q_copy(1, 1, plane(2), 3).start()

    @pl.when(p == 2)
    def _():
        arrive(1, 3)
        kv_copy(kv_of(0), 2, me.sibling(), 0).wait_send()
        q_copy(0, 2, plane(0), 2).start()

    @pl.when(p == 3)
    def _():
        arrive(2)
        q_copy(0, 3, plane(1), 2).start()
        kv_copy(kv_of(0), 3, plane(1), 0).start()

    whole(one)

    @pl.when(p == 0)
    def _():
        pair(1, 1, True)

    def second(i, c):
        q = jnp.where(p == 0, 1, jnp.where(p == 2, 2, 3))
        b = jnp.where(p == 0, 0, jnp.where(p == 1, 1 + i, jnp.where(p == 2, 1, 2)))
        pair(q, b, False)
        return c

    lax.fori_loop(0, jnp.where(p == 1, 2, 1), second, 0)

    @pl.when(p == 0)
    def _():
        hand_over(1)
        hand_over(0)
        kv_copy(kv_of(1), 0, me.sibling(), 0).wait_send()
        q_copy(1, 0, plane(2), 2).start()
        got_query(2)

    @pl.when(p == 1)
    def _():
        arrive(0)

    @pl.when(p == 2)
    def _():
        arrive(0, 3)
        got_query(1)

    @pl.when(p == 3)
    def _():
        arrive(1)

    @pl.when(p != 0)
    def _():
        whole(jnp.where(p == 3, 1, 0))

    trade_wo.wait_recv()
    ring_a.start()
    def third(i, c):
        q = jnp.where(p == 0, 2, jnp.where(p == 2, 1 + i, 3))
        b = jnp.where(p == 0, i, jnp.where(p == 3, 1, 0))
        pair(q, b, False)
        return c

    lax.fori_loop(0, 2 - last, third, 0)

    @pl.when(p == 0)
    def _():
        arrive(2)
        whole(2)

    @pl.when(p == 1)
    def _():
        arrive(3)
        whole(3)

    @pl.when(p == 2)
    def _():
        hand_over(2)
        pair(1, 1, True)
        hand_over(1)
        got_query(0)

    @pl.when(p != 3)
    def _():
        q = jnp.where(p == 0, 2, jnp.where(p == 1, 3, 0))
        pair(q, q, True)

    @pl.when(p == 3)
    def _():
        arrive(0)
        whole(0)
        pair(3, 0, False)

    @pl.when(p == 0)
    def _():
        hand_over(2)

    @pl.when(p == 2)
    def _():
        hand_over(0)

    @pl.when(last == 1)
    def _():
        hand_over(3)

    def handed(head, column):
        pltpu.make_async_remote_copy(
            heads_out.at[0, pl.ds(0, TOK)], place, hand_send.at[0], hand_recv.at[2 * head + column],
            device_id=me.sibling(), device_id_type=MESH,
        ).wait_recv()

    def block_out(half, xh, y):
        early = lax.div(lax.rem(me.z + 8 - 2 * xh, 4), 2)
        return merged.at[xh * 4 + y, early + half * (1 - 2 * early)]

    gather = HeadGather(sends, me, block_out)
    ring_b.start()

    @pl.when(p == 1)
    def _():
        handed(mine, 0)

    handed(mine, 1)
    gather.start_a()
    ring_a.take_ahead(1)
    ring_a.take_back(1)
    handed(1 - mine, 0)
    handed(1 - mine, 1)
    gather.start_b()
    ring_b.take_ahead(1)
    ring_b.take_back(1)
    gather.step_1()
    gather.step_2()
    ring_a.take_ahead(2)
    ring_a.take_back(2)
    ring_b.take_ahead(2)
    ring_b.take_back(2)
    gather.step_3()
    ring_a.take_ahead(3)
    ring_a.take_back(3)
    ring_b.take_ahead(3)
    ring_b.take_back(3)
    gather.finish()

    def merge(step, so_far):
        h = lax.rem(me.z + 8 + step, 8)
        for half in range(2):
            left = jnp.concatenate([merged[h, 0, half], merged[h, 1, half]], axis=1)
            so_far = so_far + jnp.dot(
                left, wo[h, half].reshape(256, 512), preferred_element_type=F32
            )
        return so_far

    def ready(key):
        ring_a.wait_shared(key)
        ring_b.wait_shared(key)

    ready("own")
    result = merge(0, jnp.zeros((TOK, 512), F32))
    for s in (1, 2):
        ready(("a", s))
        ready(("b", s))
        result = merge(-s, merge(s, result))
    ring_a.take_ahead(4)
    ready(("a", 3))
    ready(("b", 3))
    result = merge(-3, merge(3, result))
    ring_b.take_ahead(4)
    ready(("a", 4))
    out_ref[...] = merge(4, result).astype(BF16)

    q_copy(0, 0, me.sibling(), 2).wait_send()

    @pl.when(last == 1)
    def _():
        kv_copy(kv_of(0), 0, me.sibling(), 0).wait_send()

    @pl.when((p == 1) | (p == 2))
    def _():
        kv_copy(kv_of(0), 0, me.sibling(), 1).wait_send()

    @pl.when(p == 1)
    def _():
        q_copy(0, 0, me.sibling(), 3).wait_send()
        kv_copy(kv_of(0), 0, me.sibling(), 6).wait_send()

    @pl.when(p == 2)
    def _():
        kv_copy(kv_of(0), 0, me.sibling(), 4).wait_send()
        kv_copy(kv_of(0), 0, me.sibling(), 5).wait_send()

    for b in range(3):
        share(b, kv_of(0)).wait_send()

    @pl.when(last == 1)
    def _():
        share(3, kv_of(0)).wait_send()
        hand_copy(3, 0, partner_x, 1).wait_send()

    @pl.when(p == 1)
    def _():
        hand_copy(3, 0, me.x, 0).wait_send()

    @pl.when(last == 0)
    def _():
        for b in range(3):
            hand_copy(b, 0, partner_x, 1).wait_send()

            @pl.when(b != p)
            def _():
                hand_copy(b, 0, me.x, 0).wait_send()

    sends.finish()


def layer(tokens, wq, wk, wv, wo, down, up, angles):
    slots = 120
    any_spec = pl.BlockSpec(memory_space=pl.ANY)
    vmem = pl.BlockSpec(memory_space=pltpu.VMEM)
    return pl.pallas_call(
        layer_kernel,
        out_shape=jax.ShapeDtypeStruct((TOK, 512), BF16),
        in_specs=[any_spec] * 8,
        out_specs=vmem,
        scratch_shapes=[
            pltpu.VMEM((24, D), BF16),
            pltpu.VMEM((24, 512), BF16),
            pltpu.VMEM((2, 288, HEAD), F32),
            pltpu.VMEM((2, 512, HEAD), F32),
            pltpu.VMEM((8, 2, TOK, 512), BF16),
            pltpu.VMEM((3, 8, 2, 2, 128, 256), BF16),
            pltpu.VMEM((3, 512, 256), F32),
            pltpu.VMEM((512, 24), F32),
            pltpu.VMEM((2, 3, 512, HEAD), BF16),
            pltpu.VMEM((4, 512, HEAD), BF16),
            pltpu.VMEM((4, 2, 2, 512, HEAD), BF16),
            pltpu.VMEM((4, 512, HEAD), F32),
            pltpu.VMEM((4, 512, 1), F32),
            pltpu.VMEM((4, 512, 1), F32),
            pltpu.VMEM((4, 512, HEAD), BF16),
            pltpu.VMEM((8, 2, 2, TOK, HEAD), BF16),
            pltpu.VMEM((8, 2, 2, 128, 512), BF16),
            pltpu.SemaphoreType.DMA((slots,)),
            pltpu.SemaphoreType.DMA((slots,)),
            pltpu.SemaphoreType.DMA((12,)),
            pltpu.SemaphoreType.DMA((12,)),
            pltpu.SemaphoreType.DMA((8,)),
            pltpu.SemaphoreType.DMA((4,)),
            pltpu.SemaphoreType.DMA((8,)),
        ],
        compiler_params=pltpu.CompilerParams(
            collective_id=0, has_side_effects=True, vmem_limit_bytes=60 << 20
        ),
        name="layer",
    )(tokens, wq, wk, wv, wo, down, up, angles)


def rotary_tables():
    rows = np.concatenate([np.arange(TOK), np.arange(32) * TOK]).astype(np.float64)
    inverse_freq = 10000.0 ** (-(np.arange(HEAD // 2) * 2.0) / HEAD)
    angle = rows[:, None] * np.concatenate([inverse_freq, inverse_freq])[None, :]
    return np.stack([np.cos(angle), np.sin(angle)]).astype(np.float32)


def per_device(tokens, wq, wk, wv, wo, down, up):
    return layer(tokens, wq, wk, wv, wo, down.reshape(24, D), up.reshape(24, 512), jnp.asarray(rotary_tables()))


def solution(mesh):
    placed = P("ctx", "head")
    return jax.shard_map(
        per_device,
        mesh=mesh,
        in_specs=(placed,) * 5 + (P(), P(None, None, "head")),
        out_specs=placed,
        check_vma=False,
    )
```

```python
import functools

import jax
import jax.numpy as jnp
import numpy as np
from jax import lax
from jax.experimental import pallas as pl
from jax.experimental.pallas import tpu as pltpu
from jax.sharding import PartitionSpec as P

D = 4096
HEADS = 32
HEAD = 128
TOK = 256
MESH = pl.DeviceIdType.MESH
BF16 = jnp.bfloat16
F32 = jnp.float32


class Place:
    def __init__(self):
        c = lax.axis_index("ctx")
        h = lax.axis_index("head")
        self.z = lax.div(c, 4)
        self.xl = lax.rem(lax.div(c, 2), 2)
        self.k = lax.rem(c, 2)
        self.xh = lax.div(h, 4)
        self.y = lax.rem(h, 4)
        self.x = self.xh * 2 + self.xl
        self.h = h
        self.sigma = 1 - 2 * self.k

    def at(self, z=None, x=None, y=None, k=None):
        z = self.z if z is None else z
        x = self.x if x is None else x
        y = self.y if y is None else y
        k = self.k if k is None else k
        return (z * 4 + lax.rem(x, 2) * 2 + k, lax.div(x, 2) * 4 + y)

    def to_z(self, step):
        return self.at(z=lax.rem(self.z + 8 + step, 8))

    def to_x(self, step):
        return self.at(x=lax.rem(self.x + 4 + step, 4))

    def to_y(self, step):
        return self.at(y=lax.rem(self.y + 4 + step, 4))

    def sibling(self):
        return self.at(k=1 - self.k)

    def partner(self):
        return self.at(x=self.xh * 2 + 1 - self.xl)


def greet(devices):
    barrier = pltpu.get_barrier_semaphore()
    for device in devices:
        pl.semaphore_signal(barrier, inc=1, device_id=device, device_id_type=MESH)
    pl.semaphore_wait(barrier, len(devices))


class Sends:
    def __init__(self, send_sem, recv_sem):
        self.send_sem, self.recv_sem, self.count, self.open = send_sem, recv_sem, 0, []

    def slot(self):
        self.count += 1
        return self.count - 1

    def start(self, src, dst, device, slot):
        copy = pltpu.make_async_remote_copy(
            src_ref=src,
            dst_ref=dst,
            send_sem=self.send_sem.at[slot],
            recv_sem=self.recv_sem.at[slot],
            device_id=device,
            device_id_type=MESH,
        )
        copy.start()
        self.open.append(copy)
        return copy

    def finish(self):
        for copy in self.open:
            copy.wait_send()


class Ring4:
    def __init__(self, sends, me, sigma, to, block):
        self.sends, self.me, self.sigma, self.to, self.block = sends, me, sigma, to, block

    def place(self, step):
        return self.block(lax.rem(self.me + 4 + step * self.sigma, 4))

    def start(self):
        own = self.place(0)
        self.ahead = self.sends.start(own, own, self.to(self.sigma), self.sends.slot())
        self.back = self.sends.start(own, own, self.to(-self.sigma), self.sends.slot())

    def forward(self):
        self.ahead.wait_recv()
        block = self.place(-1)
        self.far = self.sends.start(block, block, self.to(self.sigma), self.sends.slot())

    def wait_back(self):
        self.back.wait_recv()

    def wait_far(self):
        self.far.wait_recv()


class PlaneGather:
    def __init__(self, sends, me, block):
        self.me, self.sends = me, sends
        s = me.sigma
        self.first = [
            Ring4(sends, me.x, s, me.to_x, lambda a: block(0, a, me.y)),
            Ring4(sends, me.y, s, me.to_y, lambda a: block(1, me.x, a)),
        ]
        self.second = [[], []]
        for step in (0, -1, 1, -2):
            x = lax.rem(me.x + 4 + step * s, 4)
            y = lax.rem(me.y + 4 + step * s, 4)
            self.second[0].append(Ring4(sends, me.y, s, me.to_y, lambda a, x=x: block(0, x, a)))
            self.second[1].append(Ring4(sends, me.x, s, me.to_x, lambda a, y=y: block(1, a, y)))

    def events(self):
        def start():
            for half in (0, 1):
                self.first[half].start()
            for half in (0, 1):
                self.second[half][0].start()

        def ahead():
            for half in (0, 1):
                self.first[half].forward()
                self.second[half][1].start()

        def back():
            for half in (0, 1):
                self.first[half].wait_back()
                self.second[half][2].start()

        def far():
            for half in (0, 1):
                self.first[half].wait_far()
                self.second[half][3].start()

        def second(i):
            def step():
                for half in (0, 1):
                    self.second[half][i].forward()

            return step

        def finish():
            for half in (0, 1):
                for ring in self.second[half]:
                    ring.wait_back()
                    ring.wait_far()

        return [start, ahead, back, second(0), far, second(1), second(2), second(3), finish]


class HeadGather:
    def __init__(self, sends, me, block):
        self.me, self.sends, self.block = me, sends, block
        far = 1 - me.xh
        self.own_a = Ring4(sends, me.y, me.sigma, me.to_y, lambda a: block(0, me.xh, a))
        self.far_a = Ring4(sends, me.y, me.sigma, me.to_y, lambda a: block(0, far, a))
        self.own_b = Ring4(sends, me.y, me.sigma, me.to_y, lambda a: block(1, me.xh, a))
        self.crossed = []

    def cross(self, half, step):
        block = self.block(half, self.me.xh, lax.rem(self.me.y + 4 + step * self.me.sigma, 4))
        self.crossed.append(
            self.sends.start(block, block, self.me.to_x(2), self.sends.slot())
        )

    def start_a(self):
        self.cross(0, 0)
        self.own_a.start()

    def start_b(self):
        self.own_b.start()
        self.cross(1, 0)

    def step_1(self):
        self.own_b.forward()
        self.cross(1, -1)
        self.own_b.wait_back()
        self.cross(1, 1)

    def step_2(self):
        self.crossed[0].wait_recv()
        self.far_a.start()
        self.own_a.forward()

    def step_3(self):
        self.own_b.wait_far()
        self.cross(1, -2)
        self.far_a.forward()

    def finish(self):
        for ring in (self.own_a, self.far_a):
            ring.wait_back()
            ring.wait_far()
        for copy in self.crossed[1:]:
            copy.wait_recv()


class RingZ:
    def __init__(self, sends, me, block):
        self.sends, self.me, self.block = sends, me, block
        self.ahead, self.back, self.shared = {}, {}, {}

    def place(self, step, k):
        return self.block(lax.rem(self.me.z + 8 + step, 8), k)

    def share(self, key, step):
        block = self.place(step, self.me.k)
        self.shared[key] = self.sends.start(block, block, self.me.sibling(), self.sends.slot())

    def start(self):
        me, own = self.me, self.place(0, self.me.k)
        self.ahead[1] = self.sends.start(own, own, me.to_z(me.sigma), self.sends.slot())
        self.back[1] = self.sends.start(own, own, me.to_z(-me.sigma), self.sends.slot())
        self.share("own", 0)

    def take_ahead(self, s):
        me = self.me
        self.ahead[s].wait_recv()
        if s < 4:
            block = self.place(-s * me.sigma, me.k)
            self.ahead[s + 1] = self.sends.start(block, block, me.to_z(me.sigma), self.sends.slot())
        self.share(("a", s), -s * me.sigma)

    def take_back(self, s):
        me = self.me
        self.back[s].wait_recv()
        if s < 3:
            block = self.place(s * me.sigma, me.k)
            self.back[s + 1] = self.sends.start(block, block, me.to_z(-me.sigma), self.sends.slot())
        self.share(("b", s), s * me.sigma)

    def wait_shared(self, key):
        self.shared[key].wait_recv()


def layer_kernel(
    tok_in, wq_in, wk_in, wv_in, wo_in, down_in, up_in, angle_in, out_ref,
    down_ref, up_ref, angles, turn, tok, weights, acc, low, qkv, query, kv, total, top, denom, heads_out, merged, wo,
    send_sem, recv_sem, pair_send, pair_recv, hand_send, hand_recv, local_sem,
):
    me = Place()
    w_in = (wq_in, wk_in, wv_in)
    own_cols = pl.multiple_of(me.xl * 256, 256)
    other_cols = pl.multiple_of((1 - me.xl) * 256, 256)
    p = lax.rem(me.z + 8 - 2 * me.xh, 4)
    mine = lax.div(p, 2)
    last = lax.rem(p, 2)

    def plane(q, x=None):
        return me.at(z=lax.rem(me.z + 8 - p + q, 8), x=x)

    partner_x = me.xh * 2 + 1 - me.xl
    local = [pltpu.make_async_copy(tok_in, tok.at[me.h, me.xl], local_sem.at[0])]
    for j in range(3):
        local.append(
            pltpu.make_async_copy(
                w_in[j].at[:, pl.ds(own_cols, 256)], weights.at[j, me.z, me.xl, me.k], local_sem.at[1 + j]
            )
        )
    local.append(pltpu.make_async_copy(wo_in, wo.at[me.z, me.xl, me.k], local_sem.at[4]))
    local.append(pltpu.make_async_copy(down_in, down_ref, local_sem.at[5]))
    local.append(pltpu.make_async_copy(up_in, up_ref, local_sem.at[6]))
    local.append(pltpu.make_async_copy(angle_in, angles, local_sem.at[7]))
    for copy in local:
        copy.start()
    greet(
        [
            me.to_z(1), me.to_z(-1), me.to_x(1), me.to_x(-1), me.to_x(2), me.to_y(1), me.to_y(-1), me.sibling(),
            plane(lax.rem(p + 1, 4)), plane(lax.rem(p + 2, 4)), plane(lax.rem(p + 3, 4)),
            plane(lax.rem(p + 1, 4), partner_x), plane(lax.rem(p + 2, 4), partner_x), plane(lax.rem(p + 3, 4), partner_x),
        ]
    )
    sends = Sends(send_sem, recv_sem)
    trade = []
    for j in range(3):
        trade.append(
            sends.start(
                w_in[j].at[:, pl.ds(other_cols, 256)],
                weights.at[j, me.z, me.xl, me.k],
                me.partner(),
                sends.slot(),
            )
        )
    for copy in local[1:]:
        copy.wait()
    own_ring = RingZ(sends, me, lambda z, k: weights.at[:, z, me.xl, k])
    other_ring = RingZ(sends, me, lambda z, k: weights.at[:, z, 1 - me.xl, k])
    own_ring.start()
    local[0].wait()

    def block(half, x, y):
        return tok.at[lax.div(x, 2) * 4 + y, lax.rem(x, 2), pl.ds(half * 128, 128)]

    events = PlaneGather(sends, me, block).events()
    events[0]()
    events[1]()
    for copy in trade:
        copy.wait_recv()
    other_ring.start()
    own_ring.take_ahead(1)
    own_ring.take_back(1)
    events[2]()
    events[3]()
    events[4]()
    other_ring.take_ahead(1)
    other_ring.take_back(1)
    events[5]()
    events[6]()
    own_ring.take_ahead(2)
    own_ring.take_back(2)
    events[7]()
    other_ring.take_ahead(2)
    other_ring.take_back(2)
    events[8]()
    own_ring.take_ahead(3)
    own_ring.take_back(3)
    trade_wo = sends.start(
        wo.at[me.z, me.xl, me.k], wo.at[me.z, me.xl, me.k], me.partner(), sends.slot()
    )

    def multiply(step, first=False, which=(1, 2, 0)):
        chunk = lax.rem(me.z + 8 + step, 8)
        left = tok[chunk].reshape(512, 512)
        for j in which:
            part = jnp.dot(left, weights[j, chunk].reshape(512, 256), preferred_element_type=F32)
            if first:
                acc[j] = part
            else:
                acc[j] += part

    for half in range(2):
        block_row = 256 + me.z * 4 + half * 2 + me.k
        block_cos, block_sin = angles[0, pl.ds(block_row, 1)], angles[1, pl.ds(block_row, 1)]
        row_cos, row_sin = angles[0, pl.ds(0, TOK)], angles[1, pl.ds(0, TOK)]
        turn[0, pl.ds(half * TOK, TOK)] = row_cos * block_cos - row_sin * block_sin
        lane = lax.broadcasted_iota(jnp.int32, (TOK, HEAD), 1)
        sine = row_sin * block_cos + row_cos * block_sin
        turn[1, pl.ds(half * TOK, TOK)] = jnp.where(lane < HEAD // 2, -sine, sine)

    def low_rank(chunk, so_far):
        left = tok[chunk].reshape(512, 512)
        cols = pl.multiple_of(chunk * 512, 512)
        return so_far + lax.dot_general(
            left, down_ref[:, pl.ds(cols, 512)], (((1,), (1,)), ((), ())), preferred_element_type=F32
        )

    def shared(key):
        own_ring.wait_shared(key)
        other_ring.wait_shared(key)

    shared("own")
    multiply(0, True)
    low[...] = lax.fori_loop(0, 4, low_rank, jnp.zeros((512, 24), F32))
    shared(("a", 1))
    shared(("b", 1))
    multiply(1)
    multiply(-1)
    other_ring.take_ahead(3)
    other_ring.take_back(3)
    shared(("a", 2))
    shared(("b", 2))
    multiply(2)
    multiply(-2)
    rank = lax.fori_loop(4, 8, low_rank, low[...]).astype(BF16)
    rank_of = lax.broadcasted_iota(jnp.int32, (512, 24), 1) // 8
    for j in range(3):
        part_rank = jnp.where(rank_of == j, rank, jnp.zeros_like(rank))
        acc[j] += 2.0 * jnp.dot(
            part_rank, up_ref[:, pl.ds(own_cols, 256)], preferred_element_type=F32
        )
    own_ring.take_ahead(4)
    shared(("a", 3))
    shared(("b", 3))
    multiply(3)
    multiply(-3)
    top[...] = jnp.full_like(top, -1e30)
    denom[...] = jnp.zeros_like(denom)
    total[...] = jnp.zeros_like(total)
    other_ring.take_ahead(4)
    shared(("a", 4))
    multiply(4, which=(1, 2))

    def finish_projection(j):
        for head in range(2):
            part = acc[j, :, head * HEAD : (head + 1) * HEAD]
            if j < 2:
                part = part * turn[0] + pltpu.roll(part, HEAD // 2, 1) * turn[1]
            qkv[head, j] = part.astype(BF16)

    def kv_copy(src, b, device, send):
        return pltpu.make_async_remote_copy(
            src, kv.at[b, me.k], pair_send.at[send], pair_recv.at[b],
            device_id=device, device_id_type=MESH,
        )

    def q_copy(head, b, device, send):
        return pltpu.make_async_remote_copy(
            qkv.at[head, 0], query.at[b], pair_send.at[send], pair_recv.at[4 + b],
            device_id=device, device_id_type=MESH,
        )

    def kv_of(head):
        return qkv.at[head, pl.ds(1, 2)]

    def share(b, src):
        return pltpu.make_async_remote_copy(
            src, kv.at[b, me.k], pair_send.at[8 + b], pair_recv.at[8 + b],
            device_id=me.sibling(), device_id_type=MESH,
        )

    finish_projection(1)
    finish_projection(2)

    @pl.when(p == 0)
    def _():
        kv_copy(kv_of(0), 0, plane(1), 1).start()

    @pl.when(p == 1)
    def _():
        kv_copy(kv_of(1), 1, plane(2), 1).start()

    @pl.when(p == 2)
    def _():
        kv_copy(kv_of(0), 2, plane(1), 0).start()
        kv_copy(kv_of(1), 2, plane(3), 1).start()

    share(p, kv_of(mine)).start()
    multiply(4, which=(0,))
    finish_projection(0)

    @pl.when(p == 1)
    def _():
        q_copy(0, 1, plane(0), 2).start()
        kv_copy(kv_of(0), 1, plane(0), 0).start()

    @pl.when(p != 1)
    def _():
        query[p] = qkv[mine, 0]

    kv[p, me.k] = qkv[mine, 1:3]
    ring_a = RingZ(sends, me, lambda z, k: wo.at[z, me.xl, k])
    ring_b = RingZ(sends, me, lambda z, k: wo.at[z, 1 - me.xl, k])
    scale = HEAD ** (-0.5)

    def allowed(half, core, keys):
        rows = lax.broadcasted_iota(jnp.int32, (TOK, keys), 0)
        cols = lax.broadcasted_iota(jnp.int32, (TOK, keys), 1)
        place = cols + jnp.where(cols >= TOK, 256, 0)
        return place + core * 256 <= rows + half * 512 + me.k * 256

    def pair(slot, b, diagonal):
        parts = [pl.ds(half * TOK, TOK) for half in range(2)]
        lengths = [TOK if diagonal and half == 0 else 2 * TOK for half in range(2)]
        scores = []
        for half in range(2):
            for core in range(2):
                score = lax.dot_general(
                    query[slot, parts[half]],
                    kv[b, core, 0, pl.ds(0, lengths[half])],
                    (((1,), (1,)), ((), ())),
                    preferred_element_type=F32,
                ) * scale
                if diagonal:
                    score = jnp.where(allowed(half, core, lengths[half]), score, -1e30)
                scores.append(score)
        olds = [top[slot, part] for part in parts]
        news, factors, probs = [], [], []
        for half in range(2):
            one, two = scores[2 * half : 2 * half + 2]
            news.append(jnp.maximum(olds[half], jnp.max(jnp.maximum(one, two), axis=1, keepdims=True)))
            factors.append(jnp.exp(olds[half] - news[half]))
            for core in range(2):
                prob = jnp.exp(scores[2 * half + core] - news[half])
                if diagonal:
                    prob = jnp.where(allowed(half, core, lengths[half]), prob, 0.0)
                probs.append(prob)
        sums = [
            denom[slot, parts[half]] * factors[half]
            + jnp.sum(probs[2 * half] + probs[2 * half + 1], axis=1, keepdims=True)
            for half in range(2)
        ]
        results = []
        for half in range(2):
            result = total[slot, parts[half]] * factors[half]
            for core in range(2):
                result = result + jnp.dot(
                    probs[2 * half + core].astype(BF16),
                    kv[b, core, 1, pl.ds(0, lengths[half])],
                    preferred_element_type=F32,
                )
            results.append(result)
        for half in range(2):
            top[slot, parts[half]] = news[half]
            denom[slot, parts[half]] = sums[half]
            total[slot, parts[half]] = results[half]

    def rows_of(r):
        return pl.ds(pl.multiple_of(r * TOK, TOK), TOK)

    place = merged.at[me.h, mine, me.xl]

    def hand_copy(b, r, x, column):
        return pltpu.make_async_remote_copy(
            heads_out.at[b, rows_of(r)], place, hand_send.at[2 * b + column], hand_recv.at[2 * mine + column],
            device_id=plane(b, x), device_id_type=MESH,
        )

    def hand_over(b):
        heads_out[b] = (total[b] / denom[b]).astype(BF16)
        hand_copy(b, 1 - me.xl, partner_x, 1).start()

        @pl.when(b != p)
        def _():
            hand_copy(b, me.xl, me.x, 0).start()

        @pl.when(b == p)
        def _():
            merged[me.h, mine, me.xl] = heads_out[p, rows_of(me.xl)]

    def arrive(b, onward=None):
        kv_copy(kv.at[b, me.k], b, me.sibling(), 0).wait_recv()
        if onward is not None:
            kv_copy(kv.at[b, me.k], b, plane(onward), 4 + b).start()
        share(b, kv.at[b, me.k]).start()

    def got_query(b):
        q_copy(0, b, me.sibling(), 2).wait_recv()

    def whole(b):
        share(b, kv.at[b, me.k]).wait_recv()

    def pairs(first, count, b):
        def one(i, c):
            pair(first + i, b, False)
            return c

        lax.fori_loop(0, count, one, 0)

    whole(p)

    @pl.when(p != 1)
    def _():
        pair(p, p, True)

    one = 1 + last

    @pl.when(p == 0)
    def _():
        kv_copy(kv_of(0), 0, me.sibling(), 1).wait_send()
        kv_copy(kv_of(1), 0, plane(2), 0).start()
        arrive(1)
        got_query(1)

    @pl.when(p == 1)
    def _():
        arrive(2, 0)
        got_query(3)
        q_copy(1, 1, plane(2), 3).start()

    @pl.when(p == 2)
    def _():
        arrive(1, 3)
        kv_copy(kv_of(0), 2, me.sibling(), 0).wait_send()
        q_copy(0, 2, plane(0), 2).start()

    @pl.when(p == 3)
    def _():
        arrive(2)
        q_copy(0, 3, plane(1), 2).start()
        kv_copy(kv_of(0), 3, plane(1), 0).start()

    whole(one)

    @pl.when(p == 0)
    def _():
        pair(1, 1, True)

    def second(i, c):
        q = jnp.where(p == 0, 1, jnp.where(p == 2, 2, 3))
        b = jnp.where(p == 0, 0, jnp.where(p == 1, 1 + i, jnp.where(p == 2, 1, 2)))
        pair(q, b, False)
        return c

    lax.fori_loop(0, jnp.where(p == 1, 2, 1), second, 0)

    @pl.when(p == 0)
    def _():
        hand_over(1)
        hand_over(0)
        kv_copy(kv_of(1), 0, me.sibling(), 0).wait_send()
        q_copy(1, 0, plane(2), 2).start()
        got_query(2)

    @pl.when(p == 1)
    def _():
        arrive(0)

    @pl.when(p == 2)
    def _():
        arrive(0, 3)
        got_query(1)

    @pl.when(p == 3)
    def _():
        arrive(1)

    @pl.when(p != 0)
    def _():
        whole(jnp.where(p == 3, 1, 0))

    trade_wo.wait_recv()
    ring_a.start()
    def third(i, c):
        q = jnp.where(p == 0, 2, jnp.where(p == 2, 1 + i, 3))
        b = jnp.where(p == 0, i, jnp.where(p == 3, 1, 0))
        pair(q, b, False)
        return c

    lax.fori_loop(0, 2 - last, third, 0)

    @pl.when(p == 0)
    def _():
        arrive(2)
        whole(2)

    @pl.when(p == 1)
    def _():
        arrive(3)
        whole(3)

    @pl.when(p == 2)
    def _():
        hand_over(2)
        pair(1, 1, True)
        hand_over(1)
        got_query(0)

    @pl.when(p != 3)
    def _():
        q = jnp.where(p == 0, 2, jnp.where(p == 1, 3, 0))
        pair(q, q, True)

    @pl.when(p == 3)
    def _():
        arrive(0)
        whole(0)
        pair(3, 0, False)

    @pl.when(p == 0)
    def _():
        hand_over(2)

    @pl.when(p == 2)
    def _():
        hand_over(0)

    @pl.when(last == 1)
    def _():
        hand_over(3)

    def handed(head, column):
        pltpu.make_async_remote_copy(
            heads_out.at[0, pl.ds(0, TOK)], place, hand_send.at[0], hand_recv.at[2 * head + column],
            device_id=me.sibling(), device_id_type=MESH,
        ).wait_recv()

    def block_out(half, xh, y):
        early = lax.div(lax.rem(me.z + 8 - 2 * xh, 4), 2)
        return merged.at[xh * 4 + y, early + half * (1 - 2 * early)]

    gather = HeadGather(sends, me, block_out)

    @pl.when(p == 1)
    def _():
        handed(mine, 0)

    handed(mine, 1)
    gather.start_a()
    ring_b.start()
    ring_a.take_ahead(1)
    ring_a.take_back(1)
    handed(1 - mine, 0)
    handed(1 - mine, 1)
    gather.start_b()
    ring_b.take_ahead(1)
    ring_b.take_back(1)
    gather.step_1()
    gather.step_2()
    ring_a.take_ahead(2)
    ring_a.take_back(2)
    ring_b.take_ahead(2)
    ring_b.take_back(2)
    gather.step_3()
    ring_a.take_ahead(3)
    ring_a.take_back(3)
    ring_b.take_ahead(3)
    ring_b.take_back(3)
    gather.finish()

    def merge(step, so_far):
        h = lax.rem(me.z + 8 + step, 8)
        for half in range(2):
            left = jnp.concatenate([merged[h, 0, half], merged[h, 1, half]], axis=1)
            so_far = so_far + jnp.dot(
                left, wo[h, half].reshape(256, 512), preferred_element_type=F32
            )
        return so_far

    def ready(key):
        ring_a.wait_shared(key)
        ring_b.wait_shared(key)

    ready("own")
    result = merge(0, jnp.zeros((TOK, 512), F32))
    for s in (1, 2):
        ready(("a", s))
        ready(("b", s))
        result = merge(-s, merge(s, result))
    ring_a.take_ahead(4)
    ready(("a", 3))
    ready(("b", 3))
    result = merge(-3, merge(3, result))
    ring_b.take_ahead(4)
    ready(("a", 4))
    out_ref[...] = merge(4, result).astype(BF16)

    q_copy(0, 0, me.sibling(), 2).wait_send()

    @pl.when(last == 1)
    def _():
        kv_copy(kv_of(0), 0, me.sibling(), 0).wait_send()

    @pl.when((p == 1) | (p == 2))
    def _():
        kv_copy(kv_of(0), 0, me.sibling(), 1).wait_send()

    @pl.when(p == 1)
    def _():
        q_copy(0, 0, me.sibling(), 3).wait_send()
        kv_copy(kv_of(0), 0, me.sibling(), 6).wait_send()

    @pl.when(p == 2)
    def _():
        kv_copy(kv_of(0), 0, me.sibling(), 4).wait_send()
        kv_copy(kv_of(0), 0, me.sibling(), 5).wait_send()

    for b in range(3):
        share(b, kv_of(0)).wait_send()

    @pl.when(last == 1)
    def _():
        share(3, kv_of(0)).wait_send()
        hand_copy(3, 0, partner_x, 1).wait_send()

    @pl.when(p == 1)
    def _():
        hand_copy(3, 0, me.x, 0).wait_send()

    @pl.when(last == 0)
    def _():
        for b in range(3):
            hand_copy(b, 0, partner_x, 1).wait_send()

            @pl.when(b != p)
            def _():
                hand_copy(b, 0, me.x, 0).wait_send()

    sends.finish()


def layer(tokens, wq, wk, wv, wo, down, up, angles):
    slots = 120
    any_spec = pl.BlockSpec(memory_space=pl.ANY)
    vmem = pl.BlockSpec(memory_space=pltpu.VMEM)
    return pl.pallas_call(
        layer_kernel,
        out_shape=jax.ShapeDtypeStruct((TOK, 512), BF16),
        in_specs=[any_spec] * 8,
        out_specs=vmem,
        scratch_shapes=[
            pltpu.VMEM((24, D), BF16),
            pltpu.VMEM((24, 512), BF16),
            pltpu.VMEM((2, 288, HEAD), F32),
            pltpu.VMEM((2, 512, HEAD), F32),
            pltpu.VMEM((8, 2, TOK, 512), BF16),
            pltpu.VMEM((3, 8, 2, 2, 128, 256), BF16),
            pltpu.VMEM((3, 512, 256), F32),
            pltpu.VMEM((512, 24), F32),
            pltpu.VMEM((2, 3, 512, HEAD), BF16),
            pltpu.VMEM((4, 512, HEAD), BF16),
            pltpu.VMEM((4, 2, 2, 512, HEAD), BF16),
            pltpu.VMEM((4, 512, HEAD), F32),
            pltpu.VMEM((4, 512, 1), F32),
            pltpu.VMEM((4, 512, 1), F32),
            pltpu.VMEM((4, 512, HEAD), BF16),
            pltpu.VMEM((8, 2, 2, TOK, HEAD), BF16),
            pltpu.VMEM((8, 2, 2, 128, 512), BF16),
            pltpu.SemaphoreType.DMA((slots,)),
            pltpu.SemaphoreType.DMA((slots,)),
            pltpu.SemaphoreType.DMA((12,)),
            pltpu.SemaphoreType.DMA((12,)),
            pltpu.SemaphoreType.DMA((8,)),
            pltpu.SemaphoreType.DMA((4,)),
            pltpu.SemaphoreType.DMA((8,)),
        ],
        compiler_params=pltpu.CompilerParams(
            collective_id=0, has_side_effects=True, vmem_limit_bytes=60 << 20
        ),
        name="layer",
    )(tokens, wq, wk, wv, wo, down, up, angles)


def rotary_tables():
    rows = np.concatenate([np.arange(TOK), np.arange(32) * TOK]).astype(np.float64)
    inverse_freq = 10000.0 ** (-(np.arange(HEAD // 2) * 2.0) / HEAD)
    angle = rows[:, None] * np.concatenate([inverse_freq, inverse_freq])[None, :]
    return np.stack([np.cos(angle), np.sin(angle)]).astype(np.float32)


def per_device(tokens, wq, wk, wv, wo, down, up):
    return layer(tokens, wq, wk, wv, wo, down.reshape(24, D), up.reshape(24, 512), jnp.asarray(rotary_tables()))


def solution(mesh):
    placed = P("ctx", "head")
    return jax.shard_map(
        per_device,
        mesh=mesh,
        in_specs=(placed,) * 5 + (P(), P(None, None, "head")),
        out_specs=placed,
        check_vma=False,
    )
```
